32 devices in a mesh: grp: 4 (over y, core), blk: 8 (over z, x).
Axes of the slice: x: 2, y: 2, z: 4, core: 2. Of those that a mesh axis runs over, the one named last changes fastest.
Arguments:
- child_field: bfloat16 [32768, 384], P(('grp', 'blk')), may hold values from -6 to 6
- child_weight: bfloat16 [32768], P(('grp', 'blk')), may hold values from 0.099609375 to 0.5
- child_slot: int32 [32768], P(('grp', 'blk')), may hold values from 0 to 639, as said below
- send_list: int32 [32, 640], P(('grp', 'blk')), may hold values from -1 to 255, as said below
- theta: float32 [32, 256], P('grp', 'blk'), may hold values from 0.05 to 0.24
Outputs:
- corrected: float32 [32, 256, 384], P('grp', 'blk')
The draws below stay inside these ranges and needn't reach their ends.
Inputs may be any that keep to these rules, and one draw needn't show every extreme that they name: `send_list`: row v lists, for each of its 5 nearby owners k = 0, 1, ... in turn, 128 slots: used slots first, each holding a distinct local parent number e of that owner, then -1 for unused slots; every device uses at least one slot for each nearby owner, and in every device's row one nearby owner has all 128 slots used. `child_slot`: A child's slot is k * 128 + position and is a used slot of its device's row of send_list.
All inputs are finite; a program needn't handle non-finite values.
Results may differ from the reference program's by a relative error of at most 0.0007.
Values sent between devices are 32-bit elements; how exact they have to be, the bound alone decides.
A program may use at most 64 MiB of HBM per device.

```python
import math
import jax
import jax.numpy as jnp
from jax import lax

CC = 1024
PR = 8
PCOL = 32
HALF = 2
CAP = 128
CHANNELS = 384
NPR = 32
NPC = 256
CHILDREN = 32768
N_GRP = 4
N_BLK = 8


def slot_plan(key):
    base = jax.random.fold_in(key, 4099)
    keys = jax.random.split(base, 5)
    devices_all = N_GRP * N_BLK
    cells = PR * PCOL
    reach = 2 * HALF + 1
    upper = max(1, CAP // 4) + 1
    counts = jax.random.randint(keys[0], (devices_all, reach), 1, upper)
    fullest = jax.random.randint(keys[1], (devices_all,), 0, reach)
    owners = jnp.arange(reach)[None, :]
    counts = jnp.where(owners == fullest[:, None], CAP, counts).astype(jnp.int32)
    scores = jax.random.randint(keys[2], (devices_all, reach, cells), 0, 1 << 20) * cells + jnp.arange(cells)
    order = jnp.argsort(scores, axis=-1)[..., :CAP].astype(jnp.int32)
    used = jnp.arange(CAP)[None, None, :] < counts[..., None]
    lists = jnp.where(used, order, -1).reshape(devices_all, reach * CAP).astype(jnp.int32)
    target = jax.random.randint(keys[3], (devices_all, CC), 0, reach).astype(jnp.int32)
    limit = jnp.take_along_axis(counts, target, axis=1)
    picks = jax.random.randint(keys[4], (devices_all, CC), 0, 1 << 20) % limit
    slots = (target * CAP + picks).reshape(-1).astype(jnp.int32)
    return (lists, slots)


def draw_send_list(key, part):
    return slot_plan(key)[0]


def draw_child_slot(key, part):
    return slot_plan(key)[1]


def block_levels(own_key, dims, cuts, low, high):
    def one(position, shards_of):
        steps = jax.random.uniform(jax.random.fold_in(jax.random.fold_in(own_key, 6), position), (shards_of,), jnp.float32, low / len(cuts), high / len(cuts))
        return jnp.repeat(jnp.exp(steps), dims[position] // shards_of).reshape((-1,) + (1,) * (len(dims) - position - 1))

    gain = one(*cuts[0])
    for cut in cuts[1:]:
        gain = gain * one(*cut)
    return gain


def bell_draw(key, shape, width, most, cuts=(), held_as=jnp.bfloat16):
    entries = jax.random.normal(key, shape, jnp.float32) * width
    if len(cuts) > 0:
        entries = block_levels(key, shape, cuts, -0.22, 0.18) * entries
    return jnp.clip(entries, min=-most, max=most).astype(held_as)


def setup_inputs(seed: int = 0) -> dict:
    key_list = jax.random.split(jax.random.key(seed), 6)
    child_field = bell_draw(key_list[0], (CHILDREN, CHANNELS), 1.0, 6.0, ((0, 32),))
    child_weight = jnp.clip(jnp.exp(math.log(0.5) - 1.6133518 * jax.random.uniform(key_list[1], (CHILDREN,), jnp.float32) ** block_levels(key_list[1], (CHILDREN,), ((0, 32),), -0.2, 0.2)), 0.099609375, 0.5).astype(jnp.bfloat16)
    child_slot = draw_child_slot(jax.random.fold_in(key_list[5], 71), 0)
    send_list = draw_send_list(jax.random.fold_in(key_list[5], 71), 0)
    theta = jnp.clip(jnp.exp(math.log(0.24) - 1.5686159 * jax.random.uniform(key_list[4], (NPR, NPC), jnp.float32) ** block_levels(key_list[4], (NPR, NPC), ((0, 4), (1, 8)), -0.2, 0.2)), 0.05, 0.24)
    return {"child_field": child_field, "child_weight": child_weight, "child_slot": child_slot, "send_list": send_list, "theta": theta}


def reference(child_field, child_weight, child_slot, send_list, theta):
    cells = PR * PCOL
    fields = child_field.reshape(N_GRP, N_BLK * CC, CHANNELS)
    weights = child_weight.reshape(N_GRP, N_BLK * CC)
    slots = child_slot.reshape(N_GRP, N_BLK, CC).astype(jnp.int32)
    lists = send_list.reshape(N_GRP, N_BLK, (2 * HALF + 1) * CAP).astype(jnp.int32)

    def one_group(items):
        field, weight, slot, table = items
        entry = jnp.take_along_axis(table, slot, axis=1)
        block = jnp.arange(N_BLK, dtype=jnp.int32)[:, None]
        owner = (block + slot // CAP - HALF) % N_BLK
        parent = (owner * cells + entry).reshape(-1).astype(jnp.int32)
        terms = field.astype(jnp.float32) * weight.astype(jnp.float32)[:, None]
        sums = jax.ops.segment_sum(terms, parent, num_segments=N_BLK * cells)
        sums = sums.reshape(N_BLK, PR, PCOL, CHANNELS).transpose(1, 0, 2, 3)
        return sums.reshape(PR, N_BLK * PCOL, CHANNELS)

    restricted = lax.map(one_group, (fields, weights, slots, lists))
    restricted = restricted.reshape(N_GRP * PR, N_BLK * PCOL, CHANNELS)
    padded = jnp.pad(restricted, ((1, 1), (1, 1), (0, 0)))
    beside = padded[2:, 1:-1] + padded[:-2, 1:-1] + padded[1:-1, 2:] + padded[1:-1, :-2]
    return restricted + theta[:, :, None] * (beside - 4.0 * restricted)
```

```python
import functools

import jax
import jax.numpy as jnp
from jax import lax
from jax.experimental import pallas as pl
from jax.experimental.pallas import tpu as pltpu
from jax.sharding import PartitionSpec as P

HALF = 2
PEERS = 2 * HALF
LANES = 128
SUB = 16
LOADS = 4
MESH = pl.DeviceIdType.MESH


def kernel(
    n_grp,
    n_blk,
    prows,
    pcols,
    cap,
    head,
    field_hbm,
    weight_hbm,
    slot_hbm,
    list_hbm,
    theta_hbm,
    out_ref,
    field,
    weight,
    slot,
    lists,
    theta,
    pieces,
    arrived,
    ordered,
    numbers,
    wanted,
    weighted,
    selector,
    restricted,
    theta_wide,
    row_out,
    col_out,
    row_halo,
    col_halo,
    in_sem,
    num_send,
    num_recv,
    piece_send,
    piece_recv,
    halo_send,
    halo_recv,
    ready,
):
    g = lax.axis_index("grp")
    b = lax.axis_index("blk")
    cells = prows * pcols
    children, channels = field.shape
    chunk = LANES
    parts = 2 if head < cap else 1
    f32, bf16, i32 = jnp.float32, jnp.bfloat16, jnp.int32
    early = b < HALF
    late = b >= n_blk - HALF

    def offset(i):
        if isinstance(i, int):
            return i - HALF + (i >= HALF)
        return i - HALF + (i >= HALF).astype(i32)

    def peer(i):
        return (g, lax.rem(b + offset(i) + n_blk, n_blk))

    def inside(i):
        to = b + offset(i)
        return (to >= 0) & (to < n_blk)

    turn = jnp.where(b == 0, 2, 0) + jnp.where(b == 1, 1, 0)
    turn = turn + jnp.where(b == n_blk - 2, 3, 0) + jnp.where(b == n_blk - 1, 2, 0)

    def nth(j):
        return lax.rem(turn + j, PEERS)

    barrier = pltpu.get_barrier_semaphore()
    greeted = jnp.int32(0)
    for i in range(PEERS):

        @pl.when(inside(i) | early)
        def _():
            pl.semaphore_signal(barrier, inc=1, device_id=peer(i), device_id_type=MESH)

        greeted += (inside(i) | late).astype(i32)

    @pl.when(g > 0)
    def _():
        pl.semaphore_signal(barrier, inc=1, device_id=(g - 1, b), device_id_type=MESH)

    @pl.when(g < n_grp - 1)
    def _():
        pl.semaphore_signal(barrier, inc=1, device_id=(g + 1, b), device_id_type=MESH)

    greeted += (g > 0).astype(i32) + (g < n_grp - 1).astype(i32)

    small = [
        pltpu.make_async_copy(src, dst, in_sem.at[i])
        for i, (src, dst) in enumerate(
            [(list_hbm, lists), (slot_hbm, slot), (weight_hbm, weight), (theta_hbm, theta)]
        )
    ]
    rows = children // LOADS
    large = [
        pltpu.make_async_copy(
            field_hbm.at[pl.ds(q * rows, rows)],
            field.at[pl.ds(q * rows, rows)],
            in_sem.at[len(small) + q],
        )
        for q in range(LOADS)
    ]
    for load in [*small[:3], *large, small[3]]:
        load.start()

    @pl.when(g == 0)
    def _():
        row_halo[0] = jnp.zeros_like(row_halo[0])

    @pl.when(g == n_grp - 1)
    def _():
        row_halo[1] = jnp.zeros_like(row_halo[1])

    @pl.when(b == 0)
    def _():
        col_halo[0] = jnp.zeros_like(col_halo[0])

    @pl.when(b == n_blk - 1)
    def _():
        col_halo[1] = jnp.zeros_like(col_halo[1])

    small[0].wait()
    lane = lax.broadcasted_iota(i32, (cap, cap), 1)
    sub = lax.broadcasted_iota(i32, (cap, cap), 0)
    owned = [0, 1, 3, 4]
    table = jnp.concatenate(
        [lists[:, k * cap : (k + 1) * cap] for k in owned]
        + [jnp.full((SUB - PEERS, cap), -1, i32)],
        axis=0,
    )
    place = lax.rem(table, pcols)
    rim = (table < pcols) | (table >= cells - pcols) | (place == 0) | (place == pcols - 1)
    rim = rim & (table >= 0)
    ones = jnp.where(rim, 1.0, 0.0)
    before = jnp.dot(
        ones.astype(bf16), jnp.where(sub < lane, 1.0, 0.0).astype(bf16), preferred_element_type=f32
    )
    count = jnp.sum(ones, axis=1, keepdims=True)
    own_lane = lax.broadcasted_iota(i32, (SUB, cap), 1).astype(f32)
    position = jnp.where(rim, before, count + own_lane - before).astype(i32)
    high, low = table[:8] >> 7, table[:8] & 127
    halves = jnp.concatenate([high, low], axis=0).astype(f32).astype(bf16)
    for i in range(PEERS):
        goes = position[i : i + 1, :] == sub
        source = jnp.sum(jnp.where(goes, lane, 0), axis=1, keepdims=True)
        wanted[i] = jnp.broadcast_to(source + owned[i] * cap, (cap, LANES))
        moved = lax.dot_general(
            halves,
            jnp.where(goes, 1.0, 0.0).astype(bf16),
            (((1,), (1,)), ((), ())),
            preferred_element_type=f32,
        ).astype(i32)
        ordered[i] = moved[i : i + 1, :] * 128 + moved[8 + i : 9 + i, :]
    wanted[PEERS] = sub + HALF * cap

    small[1].wait()
    small[2].wait()
    slots = slot[...]
    weights = weight[...].astype(f32)

    def weigh(i, at):
        ids = wanted[i]
        for j in range(children // LANES):
            hit = jnp.where(ids == slots[j : j + 1, :], weights[j : j + 1, :], 0.0)
            weighted[at, :, j * LANES : (j + 1) * LANES] = hit.astype(bf16)

    def number_copy(i):
        return pltpu.make_async_remote_copy(
            src_ref=ordered.at[i],
            dst_ref=numbers.at[i],
            send_sem=num_send.at[i],
            recv_sem=num_recv.at[i],
            device_id=peer(i),
            device_id_type=MESH,
        )

    spans = [pl.ds(0, head), pl.ds(head, cap - head)]

    def piece_copy(i, part):
        return pltpu.make_async_remote_copy(
            src_ref=pieces.at[i, spans[part]],
            dst_ref=arrived.at[i, spans[part]],
            send_sem=piece_send.at[i, part],
            recv_sem=piece_recv.at[i, part],
            device_id=peer(i),
            device_id_type=MESH,
        )

    def tail(j):
        if parts == 2:
            piece_copy(nth(j), 1).start()

    weigh(nth(0), 0)
    for load in large:
        load.wait()
    for j in range(PEERS):
        i = nth(j)
        if j > 0:
            weigh(i, j % 2)
        pieces[i] = jnp.dot(weighted[j % 2], field[...], preferred_element_type=f32)
        if j == 0:
            pl.semaphore_wait(barrier, greeted)
            for q in range(PEERS):

                @pl.when(late & ~inside(q))
                def _():
                    pl.semaphore_signal(
                        ready.at[q], inc=1, device_id=peer(q), device_id_type=MESH
                    )

        @pl.when(early & ~inside(i))
        def _():
            pl.semaphore_wait(ready.at[PEERS - 1 - i], 1)

        number_copy(i).start()
        piece_copy(i, 0).start()
        if j == 0:

            @pl.when(late)
            def _():
                tail(0)

        if j == 1:

            @pl.when(early)
            def _():
                tail(0)
                tail(1)

    @pl.when(~late & ~early)
    def _():
        tail(0)

    @pl.when(~early)
    def _():
        tail(1)

    tail(2)
    tail(3)

    def select(i, entries):
        hit = lax.broadcasted_iota(i32, (cells, cap), 0) == entries
        hit = jnp.where(hit, 1.0, 0.0).astype(bf16)
        selector[i] = jnp.concatenate([hit, hit], axis=1)

    def split(piece):
        top = piece.astype(bf16)
        return top, (piece - top.astype(f32)).astype(bf16)

    def spread(i, rows_of):
        return jnp.dot(selector[i], jnp.concatenate(rows_of, axis=0), preferred_element_type=f32)

    select(PEERS, lists[:, HALF * cap : (HALF + 1) * cap])
    weigh(PEERS, 0)
    made = jnp.dot(weighted[0], field[...], preferred_element_type=f32)
    restricted[...] = spread(PEERS, split(made))

    small[3].wait()
    diagonal = lax.broadcasted_iota(i32, (pcols, pcols), 0) == lax.broadcasted_iota(
        i32, (pcols, pcols), 1
    )
    for r in range(prows):
        column = jnp.sum(jnp.where(diagonal, theta[r : r + 1, :], 0.0), axis=1, keepdims=True)
        theta_wide[r * pcols : (r + 1) * pcols, :] = jnp.broadcast_to(column, (pcols, chunk))

    for i in range(PEERS):
        number_copy(i).wait_recv()
        select(i, numbers[i])

    blank = [jnp.zeros((head, channels), bf16), jnp.zeros((cap - head, channels), bf16)]

    def gather(i, part):
        piece_copy(i, part).wait_recv()
        top, rest = split(arrived[i, spans[part]])
        if parts == 1:
            rows_of = [top, rest]
        elif part == 0:
            rows_of = [top, blank[1], rest, blank[1]]
        else:
            rows_of = [blank[0], top, blank[0], rest]
        restricted[...] += spread(i, rows_of)

    def row_copy(side):
        return pltpu.make_async_remote_copy(
            src_ref=row_out.at[side],
            dst_ref=row_halo.at[side],
            send_sem=halo_send.at[side],
            recv_sem=halo_recv.at[side],
            device_id=(g - 1 if side else g + 1, b),
            device_id_type=MESH,
        )

    def col_copy(side):
        return pltpu.make_async_remote_copy(
            src_ref=col_out.at[side],
            dst_ref=col_halo.at[side],
            send_sem=halo_send.at[2 + side],
            recv_sem=halo_recv.at[2 + side],
            device_id=(g, b - 1 if side else b + 1),
            device_id_type=MESH,
        )

    sends = [
        (b < n_blk - 1, col_copy, 0),
        (b > 0, col_copy, 1),
        (g < n_grp - 1, row_copy, 0),
        (g > 0, row_copy, 1),
    ]
    gets = [
        (g > 0, row_copy, 0),
        (g < n_grp - 1, row_copy, 1),
        (b > 0, col_copy, 0),
        (b < n_blk - 1, col_copy, 1),
    ]

    arrivals = [2, 3, 1, 0]
    for i in arrivals:
        gather(i, 0)
    for r in range(prows):
        col_out[0, r : r + 1] = restricted[(r + 1) * pcols - 1 : (r + 1) * pcols]
        col_out[1, r : r + 1] = restricted[r * pcols : r * pcols + 1]
    row_out[0] = restricted[cells - pcols :]
    row_out[1] = restricted[:pcols]
    for here, copy, side in sends:

        @pl.when(here)
        def _():
            copy(side).start()

    if parts == 2:
        for i in arrivals:
            gather(i, 1)

    for here, copy, side in gets:

        @pl.when(here)
        def _():
            copy(side).wait_recv()

    col = lax.rem(lax.broadcasted_iota(i32, (cells, chunk), 0), pcols)
    for c in range(channels // chunk):
        at = slice(c * chunk, (c + 1) * chunk)
        own = restricted[:, at]

        def widened(side):
            return jnp.broadcast_to(
                col_halo[side, :, at][:, None, :], (prows, pcols, chunk)
            ).reshape(cells, chunk)

        up = jnp.concatenate([row_halo[0, :, at], own[: cells - pcols]], axis=0)
        down = jnp.concatenate([own[pcols:], row_halo[1, :, at]], axis=0)
        left = jnp.where(col == 0, widened(0), pltpu.roll(own, 1, 0))
        right = jnp.where(col == pcols - 1, widened(1), pltpu.roll(own, cells - 1, 0))
        beside = down + up + right + left
        out_ref[:, at] = own + theta_wide[...] * (beside - 4.0 * own)

    for i in range(PEERS):
        number_copy(i).wait_send()
        for part in range(parts):
            piece_copy(i, part).wait_send()
    for here, copy, side in sends:

        @pl.when(here)
        def _():
            copy(side).wait_send()


def body(n_grp, n_blk, child_field, child_weight, child_slot, send_list, theta):
    children, channels = child_field.shape
    prows, pcols = theta.shape
    cells = prows * pcols
    cap = send_list.shape[1] // (PEERS + 1)
    rim = 2 * (prows + pcols) - 4
    head = min(cap, -(-rim // SUB) * SUB)
    groups = children // LANES
    f32, bf16, i32 = jnp.float32, jnp.bfloat16, jnp.int32
    dma = pltpu.SemaphoreType.DMA
    out = pl.pallas_call(
        functools.partial(kernel, n_grp, n_blk, prows, pcols, cap, head),
        out_shape=pltpu.VMEM((cells, channels), f32),
        in_specs=[pl.BlockSpec(memory_space=pltpu.HBM)] * 5,
        out_specs=pl.BlockSpec(memory_space=pltpu.VMEM),
        scratch_shapes=[
            pltpu.VMEM((children, channels), bf16),
            pltpu.VMEM((groups, LANES), bf16),
            pltpu.VMEM((groups, LANES), i32),
            pltpu.VMEM(send_list.shape, i32),
            pltpu.VMEM((prows, pcols), f32),
            pltpu.VMEM((PEERS, cap, channels), f32),
            pltpu.VMEM((PEERS, cap, channels), f32),
            pltpu.VMEM((PEERS, 1, cap), i32),
            pltpu.VMEM((PEERS, 1, cap), i32),
            pltpu.VMEM((PEERS + 1, cap, LANES), i32),
            pltpu.VMEM((2, cap, children), bf16),
            pltpu.VMEM((PEERS + 1, cells, 2 * cap), bf16),
            pltpu.VMEM((cells, channels), f32),
            pltpu.VMEM((cells, LANES), f32),
            pltpu.VMEM((2, pcols, channels), f32),
            pltpu.VMEM((2, prows, channels), f32),
            pltpu.VMEM((2, pcols, channels), f32),
            pltpu.VMEM((2, prows, channels), f32),
            dma((4 + LOADS,)),
            dma((PEERS,)),
            dma((PEERS,)),
            dma((PEERS, 2)),
            dma((PEERS, 2)),
            dma((4,)),
            dma((4,)),
            pltpu.SemaphoreType.REGULAR((PEERS,)),
        ],
        compiler_params=pltpu.CompilerParams(
            collective_id=0, has_side_effects=True, vmem_limit_bytes=32 * 1024 * 1024
        ),
        name="nest_feedback",
    )(
        *[
            pltpu.with_memory_space_constraint(x, pltpu.HBM)
            for x in (
                child_field,
                child_weight.reshape(groups, LANES),
                child_slot.reshape(groups, LANES),
                send_list,
                theta,
            )
        ]
    )
    return out.reshape(prows, pcols, channels)


def solution(mesh):
    return jax.shard_map(
        functools.partial(body, mesh.shape["grp"], mesh.shape["blk"]),
        mesh=mesh,
        in_specs=(
            P(("grp", "blk"), None),
            P(("grp", "blk")),
            P(("grp", "blk")),
            P(("grp", "blk"), None),
            P("grp", "blk"),
        ),
        out_specs=P("grp", "blk", None),
        check_vma=False,
    )
```

```python
import functools

import jax
import jax.numpy as jnp
from jax import lax
from jax.experimental import pallas as pl
from jax.experimental.pallas import tpu as pltpu
from jax.sharding import PartitionSpec as P

HALF = 2
PEERS = 2 * HALF
LANES = 128
SUB = 16
MESH = pl.DeviceIdType.MESH


def kernel(
    n_grp,
    n_blk,
    prows,
    pcols,
    cap,
    head,
    field_hbm,
    weight_hbm,
    slot_hbm,
    list_hbm,
    theta_hbm,
    out_ref,
    field,
    weight,
    slot,
    lists,
    theta,
    pieces,
    arrived,
    ordered,
    numbers,
    wanted,
    weighted,
    selector,
    restricted,
    theta_wide,
    row_out,
    col_out,
    row_halo,
    col_halo,
    in_sem,
    num_send,
    num_recv,
    piece_send,
    piece_recv,
    halo_send,
    halo_recv,
    ready,
):
    g = lax.axis_index("grp")
    b = lax.axis_index("blk")
    cells = prows * pcols
    children, channels = field.shape
    chunk = LANES
    parts = 2 if head < cap else 1
    f32, bf16, i32 = jnp.float32, jnp.bfloat16, jnp.int32
    early = b < HALF
    late = b >= n_blk - HALF

    def offset(i):
        if isinstance(i, int):
            return i - HALF + (i >= HALF)
        return i - HALF + (i >= HALF).astype(i32)

    def peer(i):
        return (g, lax.rem(b + offset(i) + n_blk, n_blk))

    turn = jnp.where(b == 0, 2, 0) + jnp.where(b == 1, 1, 0)
    turn = turn + jnp.where(b == n_blk - 2, 3, 0) + jnp.where(b == n_blk - 1, 2, 0)

    def nth(j):
        return lax.rem(turn + j, PEERS)

    def above(i):
        return lax.rem(b + offset(i) + n_blk, n_blk) > b

    barrier = pltpu.get_barrier_semaphore()
    greeted = (g > 0).astype(i32)
    for i in range(PEERS):

        @pl.when(above(i))
        def _():
            pl.semaphore_signal(barrier, inc=1, device_id=peer(i), device_id_type=MESH)

        greeted += 1 - above(i).astype(i32)

    @pl.when(g < n_grp - 1)
    def _():
        pl.semaphore_signal(barrier, inc=1, device_id=(g + 1, b), device_id_type=MESH)

    small = [
        pltpu.make_async_copy(src, dst, in_sem.at[i])
        for i, (src, dst) in enumerate(
            [(list_hbm, lists), (slot_hbm, slot), (weight_hbm, weight), (theta_hbm, theta)]
        )
    ]
    large = [
        pltpu.make_async_copy(
            field_hbm.at[:, pl.ds(q * chunk, chunk)],
            field.at[:, pl.ds(q * chunk, chunk)],
            in_sem.at[len(small) + q],
        )
        for q in range(channels // chunk)
    ]
    for load in [*small[:3], *large, small[3]]:
        load.start()

    @pl.when(g == 0)
    def _():
        row_halo[0] = jnp.zeros_like(row_halo[0])

    @pl.when(g == n_grp - 1)
    def _():
        row_halo[1] = jnp.zeros_like(row_halo[1])

    @pl.when(b == 0)
    def _():
        col_halo[0] = jnp.zeros_like(col_halo[0])

    @pl.when(b == n_blk - 1)
    def _():
        col_halo[1] = jnp.zeros_like(col_halo[1])

    small[0].wait()
    lane = lax.broadcasted_iota(i32, (cap, cap), 1)
    sub = lax.broadcasted_iota(i32, (cap, cap), 0)
    owned = [0, 1, 3, 4]
    table = jnp.concatenate(
        [lists[:, k * cap : (k + 1) * cap] for k in owned]
        + [jnp.full((SUB - PEERS, cap), -1, i32)],
        axis=0,
    )
    place = lax.rem(table, pcols)
    rim = (table < pcols) | (table >= cells - pcols) | (place == 0) | (place == pcols - 1)
    rim = rim & (table >= 0)
    ones = jnp.where(rim, 1.0, 0.0)
    before = jnp.dot(
        ones.astype(bf16), jnp.where(sub < lane, 1.0, 0.0).astype(bf16), preferred_element_type=f32
    )
    count = jnp.sum(ones, axis=1, keepdims=True)
    own_lane = lax.broadcasted_iota(i32, (SUB, cap), 1).astype(f32)
    position = jnp.where(rim, before, count + own_lane - before).astype(i32)
    high, low = table[:8] >> 7, table[:8] & 127
    halves = jnp.concatenate([high, low], axis=0).astype(f32).astype(bf16)
    for i in range(PEERS):
        goes = position[i : i + 1, :] == sub
        source = jnp.sum(jnp.where(goes, lane, 0), axis=1, keepdims=True)
        wanted[i] = jnp.broadcast_to(source + owned[i] * cap, (cap, LANES))
        moved = lax.dot_general(
            halves,
            jnp.where(goes, 1.0, 0.0).astype(bf16),
            (((1,), (1,)), ((), ())),
            preferred_element_type=f32,
        ).astype(i32)
        ordered[i] = moved[i : i + 1, :] * 128 + moved[8 + i : 9 + i, :]
    wanted[PEERS] = sub + HALF * cap

    small[1].wait()
    small[2].wait()
    slots = slot[...]
    weights = weight[...].astype(f32)

    def weigh(i, at):
        ids = wanted[i]
        for j in range(children // LANES):
            hit = jnp.where(ids == slots[j : j + 1, :], weights[j : j + 1, :], 0.0)
            weighted[at, :, j * LANES : (j + 1) * LANES] = hit.astype(bf16)

    def number_copy(i):
        return pltpu.make_async_remote_copy(
            src_ref=ordered.at[i],
            dst_ref=numbers.at[i],
            send_sem=num_send.at[i],
            recv_sem=num_recv.at[i],
            device_id=peer(i),
            device_id_type=MESH,
        )

    spans = [pl.ds(0, head), pl.ds(head, cap - head)]

    def piece_copy(i, part):
        return pltpu.make_async_remote_copy(
            src_ref=pieces.at[i, spans[part]],
            dst_ref=arrived.at[i, spans[part]],
            send_sem=piece_send.at[i, part],
            recv_sem=piece_recv.at[i, part],
            device_id=peer(i),
            device_id_type=MESH,
        )

    def first_copy(i, start):
        at = pl.ds(start, chunk)
        return pltpu.make_async_remote_copy(
            src_ref=pieces.at[i, spans[0], at],
            dst_ref=arrived.at[i, spans[0], at],
            send_sem=piece_send.at[i, 0],
            recv_sem=piece_recv.at[i, 0],
            device_id=peer(i),
            device_id_type=MESH,
        )

    def tail(j):
        if parts == 2:
            piece_copy(nth(j), 1).start()

    @pl.when(greeted > 0)
    def _():
        pl.semaphore_wait(barrier, greeted)

    for q in range(PEERS):

        @pl.when(~above(q))
        def _():
            pl.semaphore_signal(
                ready.at[q], inc=1, device_id=peer(q), device_id_type=MESH
            )

    @pl.when(g > 0)
    def _():
        pl.semaphore_signal(
            ready.at[PEERS], inc=1, device_id=(g - 1, b), device_id_type=MESH
        )

    weigh(nth(0), 0)
    for j in range(PEERS):
        i = nth(j)
        if j > 0:
            weigh(i, j % 2)
            pieces[i] = jnp.dot(weighted[j % 2], field[...], preferred_element_type=f32)
        @pl.when(above(i))
        def _():
            pl.semaphore_wait(ready.at[PEERS - 1 - i], 1)

        number_copy(i).start()
        if j > 0:
            piece_copy(i, 0).start()
        else:
            for q, load in enumerate(large):
                load.wait()
                at = slice(q * chunk, (q + 1) * chunk)
                pieces[i, :, at] = jnp.dot(weighted[0], field[:, at], preferred_element_type=f32)
                first_copy(i, q * chunk).start()
        if j == 1:

            @pl.when((b == n_blk - 1) & (lax.rem(g, 2) == 0))
            def _():
                tail(0)

    @pl.when(~((b == n_blk - 1) & (lax.rem(g, 2) == 0)))
    def _():
        tail(0)

    for j in range(1, PEERS):
        tail(j)

    def select(i, entries):
        hit = lax.broadcasted_iota(i32, (cells, cap), 0) == entries
        hit = jnp.where(hit, 1.0, 0.0).astype(bf16)
        selector[i] = jnp.concatenate([hit, hit], axis=1)

    def split(piece):
        top = piece.astype(bf16)
        return top, (piece - top.astype(f32)).astype(bf16)

    def spread(i, rows_of):
        return jnp.dot(selector[i], jnp.concatenate(rows_of, axis=0), preferred_element_type=f32)

    select(PEERS, lists[:, HALF * cap : (HALF + 1) * cap])
    weigh(PEERS, 0)
    made = jnp.dot(weighted[0], field[...], preferred_element_type=f32)
    restricted[...] = spread(PEERS, split(made))

    small[3].wait()
    diagonal = lax.broadcasted_iota(i32, (pcols, pcols), 0) == lax.broadcasted_iota(
        i32, (pcols, pcols), 1
    )
    for r in range(prows):
        column = jnp.sum(jnp.where(diagonal, theta[r : r + 1, :], 0.0), axis=1, keepdims=True)
        theta_wide[r * pcols : (r + 1) * pcols, :] = jnp.broadcast_to(column, (pcols, chunk))

    for i in range(PEERS):
        number_copy(i).wait_recv()
        select(i, numbers[i])

    blank = [jnp.zeros((head, channels), bf16), jnp.zeros((cap - head, channels), bf16)]

    def gather(i, part):
        piece_copy(i, part).wait_recv()
        top, rest = split(arrived[i, spans[part]])
        if parts == 1:
            rows_of = [top, rest]
        elif part == 0:
            rows_of = [top, blank[1], rest, blank[1]]
        else:
            rows_of = [blank[0], top, blank[0], rest]
        restricted[...] += spread(i, rows_of)

    def row_copy(side):
        return pltpu.make_async_remote_copy(
            src_ref=row_out.at[side],
            dst_ref=row_halo.at[side],
            send_sem=halo_send.at[side],
            recv_sem=halo_recv.at[side],
            device_id=(g - 1 if side else g + 1, b),
            device_id_type=MESH,
        )

    def col_copy(side):
        return pltpu.make_async_remote_copy(
            src_ref=col_out.at[side],
            dst_ref=col_halo.at[side],
            send_sem=halo_send.at[2 + side],
            recv_sem=halo_recv.at[2 + side],
            device_id=(g, b - 1 if side else b + 1),
            device_id_type=MESH,
        )

    sends = [
        (b < n_blk - 1, col_copy, 0),
        (b > 0, col_copy, 1),
        (g < n_grp - 1, row_copy, 0),
        (g > 0, row_copy, 1),
    ]
    gets = [
        (g > 0, row_copy, 0),
        (g < n_grp - 1, row_copy, 1),
        (b > 0, col_copy, 0),
        (b < n_blk - 1, col_copy, 1),
    ]

    arrivals = [2, 3, 1, 0]
    for i in arrivals:
        gather(i, 0)
    for r in range(prows):
        col_out[0, r : r + 1] = restricted[(r + 1) * pcols - 1 : (r + 1) * pcols]
        col_out[1, r : r + 1] = restricted[r * pcols : r * pcols + 1]
    row_out[0] = restricted[cells - pcols :]
    row_out[1] = restricted[:pcols]
    @pl.when(g < n_grp - 1)
    def _():
        pl.semaphore_wait(ready.at[PEERS], 1)

    for here, copy, side in sends:

        @pl.when(here)
        def _():
            copy(side).start()

    if parts == 2:
        for i in arrivals:
            gather(i, 1)

    for here, copy, side in gets:

        @pl.when(here)
        def _():
            copy(side).wait_recv()

    col = lax.rem(lax.broadcasted_iota(i32, (cells, chunk), 0), pcols)
    for c in range(channels // chunk):
        at = slice(c * chunk, (c + 1) * chunk)
        own = restricted[:, at]

        def widened(side):
            return jnp.broadcast_to(
                col_halo[side, :, at][:, None, :], (prows, pcols, chunk)
            ).reshape(cells, chunk)

        up = jnp.concatenate([row_halo[0, :, at], own[: cells - pcols]], axis=0)
        down = jnp.concatenate([own[pcols:], row_halo[1, :, at]], axis=0)
        left = jnp.where(col == 0, widened(0), pltpu.roll(own, 1, 0))
        right = jnp.where(col == pcols - 1, widened(1), pltpu.roll(own, cells - 1, 0))
        beside = down + up + right + left
        out_ref[:, at] = own + theta_wide[...] * (beside - 4.0 * own)

    for i in range(PEERS):
        number_copy(i).wait_send()
        for part in range(parts):
            piece_copy(i, part).wait_send()
    for here, copy, side in sends:

        @pl.when(here)
        def _():
            copy(side).wait_send()


def body(n_grp, n_blk, child_field, child_weight, child_slot, send_list, theta):
    children, channels = child_field.shape
    prows, pcols = theta.shape
    cells = prows * pcols
    cap = send_list.shape[1] // (PEERS + 1)
    rim = 2 * (prows + pcols) - 4
    head = min(cap, -(-rim // SUB) * SUB)
    groups = children // LANES
    f32, bf16, i32 = jnp.float32, jnp.bfloat16, jnp.int32
    dma = pltpu.SemaphoreType.DMA
    out = pl.pallas_call(
        functools.partial(kernel, n_grp, n_blk, prows, pcols, cap, head),
        out_shape=pltpu.VMEM((cells, channels), f32),
        in_specs=[pl.BlockSpec(memory_space=pltpu.HBM)] * 5,
        out_specs=pl.BlockSpec(memory_space=pltpu.VMEM),
        scratch_shapes=[
            pltpu.VMEM((children, channels), bf16),
            pltpu.VMEM((groups, LANES), bf16),
            pltpu.VMEM((groups, LANES), i32),
            pltpu.VMEM(send_list.shape, i32),
            pltpu.VMEM((prows, pcols), f32),
            pltpu.VMEM((PEERS, cap, channels), f32),
            pltpu.VMEM((PEERS, cap, channels), f32),
            pltpu.VMEM((PEERS, 1, cap), i32),
            pltpu.VMEM((PEERS, 1, cap), i32),
            pltpu.VMEM((PEERS + 1, cap, LANES), i32),
            pltpu.VMEM((2, cap, children), bf16),
            pltpu.VMEM((PEERS + 1, cells, 2 * cap), bf16),
            pltpu.VMEM((cells, channels), f32),
            pltpu.VMEM((cells, LANES), f32),
            pltpu.VMEM((2, pcols, channels), f32),
            pltpu.VMEM((2, prows, channels), f32),
            pltpu.VMEM((2, pcols, channels), f32),
            pltpu.VMEM((2, prows, channels), f32),
            dma((4 + channels // LANES,)),
            dma((PEERS,)),
            dma((PEERS,)),
            dma((PEERS, 2)),
            dma((PEERS, 2)),
            dma((4,)),
            dma((4,)),
            pltpu.SemaphoreType.REGULAR((PEERS + 1,)),
        ],
        compiler_params=pltpu.CompilerParams(
            collective_id=0, has_side_effects=True, vmem_limit_bytes=32 * 1024 * 1024
        ),
        name="nest_feedback",
    )(
        *[
            pltpu.with_memory_space_constraint(x, pltpu.HBM)
            for x in (
                child_field,
                child_weight.reshape(groups, LANES),
                child_slot.reshape(groups, LANES),
                send_list,
                theta,
            )
        ]
    )
    return out.reshape(prows, pcols, channels)


def solution(mesh):
    return jax.shard_map(
        functools.partial(body, mesh.shape["grp"], mesh.shape["blk"]),
        mesh=mesh,
        in_specs=(
            P(("grp", "blk"), None),
            P(("grp", "blk")),
            P(("grp", "blk")),
            P(("grp", "blk"), None),
            P("grp", "blk"),
        ),
        out_specs=P("grp", "blk", None),
        check_vma=False,
    )
```

```python
import functools

import jax
import jax.numpy as jnp
from jax import lax
from jax.experimental import pallas as pl
from jax.experimental.pallas import tpu as pltpu
from jax.sharding import PartitionSpec as P

HALF = 2
PEERS = 2 * HALF
LANES = 128
SUB = 16
MESH = pl.DeviceIdType.MESH


def kernel(
    n_grp,
    n_blk,
    prows,
    pcols,
    cap,
    head,
    field_hbm,
    weight_hbm,
    slot_hbm,
    list_hbm,
    theta_hbm,
    out_ref,
    field,
    weight,
    slot,
    lists,
    theta,
    pieces,
    arrived,
    ordered,
    numbers,
    wanted,
    weighted,
    selector,
    restricted,
    theta_wide,
    row_out,
    col_out,
    row_halo,
    col_halo,
    in_sem,
    num_send,
    num_recv,
    piece_send,
    piece_recv,
    halo_send,
    halo_recv,
    ready,
):
    g = lax.axis_index("grp")
    b = lax.axis_index("blk")
    cells = prows * pcols
    children, channels = field.shape
    chunk = LANES
    parts = 2 if head < cap else 1
    f32, bf16, i32 = jnp.float32, jnp.bfloat16, jnp.int32
    early = b < HALF
    late = b >= n_blk - HALF

    def offset(i):
        if isinstance(i, int):
            return i - HALF + (i >= HALF)
        return i - HALF + (i >= HALF).astype(i32)

    def peer(i):
        return (g, lax.rem(b + offset(i) + n_blk, n_blk))

    turn = jnp.where(b == 0, 2, 0) + jnp.where(b == 1, 1, 0)
    turn = turn + jnp.where(b == n_blk - 2, 3, 0) + jnp.where(b == n_blk - 1, 2, 0)

    def nth(j):
        return lax.rem(turn + j, PEERS)

    def above(i):
        return lax.rem(b + offset(i) + n_blk, n_blk) > b

    small = [
        pltpu.make_async_copy(src, dst, in_sem.at[i])
        for i, (src, dst) in enumerate(
            [(list_hbm, lists), (slot_hbm, slot), (weight_hbm, weight), (theta_hbm, theta)]
        )
    ]
    large = [
        pltpu.make_async_copy(
            field_hbm.at[:, pl.ds(q * chunk, chunk)],
            field.at[:, pl.ds(q * chunk, chunk)],
            in_sem.at[len(small) + q],
        )
        for q in range(channels // chunk)
    ]
    for load in [*small[:3], *large, small[3]]:
        load.start()

    barrier = pltpu.get_barrier_semaphore()
    greeted = (g > 0).astype(i32)
    for i in range(PEERS):

        @pl.when(above(i))
        def _():
            pl.semaphore_signal(barrier, inc=1, device_id=peer(i), device_id_type=MESH)

        greeted += 1 - above(i).astype(i32)

    @pl.when(g < n_grp - 1)
    def _():
        pl.semaphore_signal(barrier, inc=1, device_id=(g + 1, b), device_id_type=MESH)

    @pl.when(g == 0)
    def _():
        row_halo[0] = jnp.zeros_like(row_halo[0])

    @pl.when(g == n_grp - 1)
    def _():
        row_halo[1] = jnp.zeros_like(row_halo[1])

    @pl.when(b == 0)
    def _():
        col_halo[0] = jnp.zeros_like(col_halo[0])

    @pl.when(b == n_blk - 1)
    def _():
        col_halo[1] = jnp.zeros_like(col_halo[1])

    small[0].wait()
    lane = lax.broadcasted_iota(i32, (cap, cap), 1)
    sub = lax.broadcasted_iota(i32, (cap, cap), 0)
    owned = [0, 1, 3, 4]
    table = jnp.concatenate(
        [lists[:, k * cap : (k + 1) * cap] for k in owned]
        + [jnp.full((SUB - PEERS, cap), -1, i32)],
        axis=0,
    )
    place = lax.rem(table, pcols)
    rim = (table < pcols) | (table >= cells - pcols) | (place == 0) | (place == pcols - 1)
    rim = rim & (table >= 0)
    ones = jnp.where(rim, 1.0, 0.0)
    before = jnp.dot(
        ones.astype(bf16), jnp.where(sub < lane, 1.0, 0.0).astype(bf16), preferred_element_type=f32
    )
    count = jnp.sum(ones, axis=1, keepdims=True)
    own_lane = lax.broadcasted_iota(i32, (SUB, cap), 1).astype(f32)
    position = jnp.where(rim, before, count + own_lane - before).astype(i32)
    high, low = table[:8] >> 7, table[:8] & 127
    halves = jnp.concatenate([high, low], axis=0).astype(f32).astype(bf16)
    for i in range(PEERS):
        goes = position[i : i + 1, :] == sub
        source = jnp.sum(jnp.where(goes, lane, 0), axis=1, keepdims=True)
        wanted[i] = jnp.broadcast_to(source + owned[i] * cap, (cap, LANES))
        moved = lax.dot_general(
            halves,
            jnp.where(goes, 1.0, 0.0).astype(bf16),
            (((1,), (1,)), ((), ())),
            preferred_element_type=f32,
        ).astype(i32)
        ordered[i] = moved[i : i + 1, :] * 128 + moved[8 + i : 9 + i, :]
    wanted[PEERS] = sub + HALF * cap

    small[1].wait()
    small[2].wait()
    slots = slot[...]
    weights = weight[...].astype(f32)

    def weigh(i, at):
        ids = wanted[i]
        for j in range(children // LANES):
            hit = jnp.where(ids == slots[j : j + 1, :], weights[j : j + 1, :], 0.0)
            weighted[at, :, j * LANES : (j + 1) * LANES] = hit.astype(bf16)

    def number_copy(i):
        return pltpu.make_async_remote_copy(
            src_ref=ordered.at[i],
            dst_ref=numbers.at[i],
            send_sem=num_send.at[i],
            recv_sem=num_recv.at[i],
            device_id=peer(i),
            device_id_type=MESH,
        )

    spans = [pl.ds(0, head), pl.ds(head, cap - head)]

    def piece_copy(i, part):
        return pltpu.make_async_remote_copy(
            src_ref=pieces.at[i, spans[part]],
            dst_ref=arrived.at[i, spans[part]],
            send_sem=piece_send.at[i, part],
            recv_sem=piece_recv.at[i, part],
            device_id=peer(i),
            device_id_type=MESH,
        )

    def first_copy(i, start):
        at = pl.ds(start, chunk)
        return pltpu.make_async_remote_copy(
            src_ref=pieces.at[i, spans[0], at],
            dst_ref=arrived.at[i, spans[0], at],
            send_sem=piece_send.at[i, 0],
            recv_sem=piece_recv.at[i, 0],
            device_id=peer(i),
            device_id_type=MESH,
        )

    def tail(j):
        if parts == 2:
            piece_copy(nth(j), 1).start()

    @pl.when(greeted > 0)
    def _():
        pl.semaphore_wait(barrier, greeted)

    for q in range(PEERS):

        @pl.when(~above(q))
        def _():
            pl.semaphore_signal(
                ready.at[q], inc=1, device_id=peer(q), device_id_type=MESH
            )

    @pl.when(g > 0)
    def _():
        pl.semaphore_signal(
            ready.at[PEERS], inc=1, device_id=(g - 1, b), device_id_type=MESH
        )

    weigh(nth(0), 0)
    for j in range(PEERS):
        i = nth(j)
        if j > 0:
            weigh(i, j % 2)
            pieces[i] = jnp.dot(weighted[j % 2], field[...], preferred_element_type=f32)
        @pl.when(above(i))
        def _():
            pl.semaphore_wait(ready.at[PEERS - 1 - i], 1)

        number_copy(i).start()
        if j > 0:
            piece_copy(i, 0).start()
        else:
            for q, load in enumerate(large):
                load.wait()
                at = slice(q * chunk, (q + 1) * chunk)
                pieces[i, :, at] = jnp.dot(weighted[0], field[:, at], preferred_element_type=f32)
                first_copy(i, q * chunk).start()
        if j == 1:

            @pl.when((b == n_blk - 1) & (lax.rem(g, 2) == 0))
            def _():
                tail(0)

    @pl.when(~((b == n_blk - 1) & (lax.rem(g, 2) == 0)))
    def _():
        tail(0)

    for j in range(1, PEERS):
        tail(j)

    def select(i, entries):
        hit = lax.broadcasted_iota(i32, (cells, cap), 0) == entries
        hit = jnp.where(hit, 1.0, 0.0).astype(bf16)
        selector[i] = jnp.concatenate([hit, hit], axis=1)

    def split(piece):
        top = piece.astype(bf16)
        return top, (piece - top.astype(f32)).astype(bf16)

    def spread(i, rows_of):
        return jnp.dot(selector[i], jnp.concatenate(rows_of, axis=0), preferred_element_type=f32)

    select(PEERS, lists[:, HALF * cap : (HALF + 1) * cap])
    weigh(PEERS, 0)
    made = jnp.dot(weighted[0], field[...], preferred_element_type=f32)
    restricted[...] = spread(PEERS, split(made))

    small[3].wait()
    diagonal = lax.broadcasted_iota(i32, (pcols, pcols), 0) == lax.broadcasted_iota(
        i32, (pcols, pcols), 1
    )
    for r in range(prows):
        column = jnp.sum(jnp.where(diagonal, theta[r : r + 1, :], 0.0), axis=1, keepdims=True)
        theta_wide[r * pcols : (r + 1) * pcols, :] = jnp.broadcast_to(column, (pcols, chunk))

    for i in range(PEERS):
        number_copy(i).wait_recv()
        select(i, numbers[i])

    rest = cap - head
    paired = parts == 2 and rest <= head
    if paired:
        lane8 = lax.broadcasted_iota(i32, (8, cap), 1)
        for p in range(2):
            first = jnp.broadcast_to(numbers[2 - p], (8, cap))
            second = pltpu.roll(jnp.broadcast_to(numbers[3 - 3 * p], (8, cap)), cap - rest, 1)
            both = jnp.where(lane8 >= head, first, jnp.where(lane8 >= head - rest, second, -1))
            select(PEERS + 1 + p, both[:1])

    def gather_pair(p):
        rows_of = [[], []]
        for i in (3 - 3 * p, 2 - p):
            piece_copy(i, 1).wait_recv()
            for side, value in enumerate(split(arrived[i, spans[1]])):
                rows_of[side].append(value)
        if head > rest:
            gap = [jnp.zeros((head - rest, channels), bf16)]
        else:
            gap = []
        restricted[...] += spread(PEERS + 1 + p, [*gap, *rows_of[0], *gap, *rows_of[1]])

    blank = [jnp.zeros((head, channels), bf16), jnp.zeros((cap - head, channels), bf16)]

    def gather(i, part):
        piece_copy(i, part).wait_recv()
        top, rest = split(arrived[i, spans[part]])
        if parts == 1:
            rows_of = [top, rest]
        elif part == 0:
            rows_of = [top, blank[1], rest, blank[1]]
        else:
            rows_of = [blank[0], top, blank[0], rest]
        restricted[...] += spread(i, rows_of)

    def row_copy(side):
        return pltpu.make_async_remote_copy(
            src_ref=row_out.at[side],
            dst_ref=row_halo.at[side],
            send_sem=halo_send.at[side],
            recv_sem=halo_recv.at[side],
            device_id=(g - 1 if side else g + 1, b),
            device_id_type=MESH,
        )

    def col_copy(side):
        return pltpu.make_async_remote_copy(
            src_ref=col_out.at[side],
            dst_ref=col_halo.at[side],
            send_sem=halo_send.at[2 + side],
            recv_sem=halo_recv.at[2 + side],
            device_id=(g, b - 1 if side else b + 1),
            device_id_type=MESH,
        )

    sends = [
        (b < n_blk - 1, col_copy, 0),
        (b > 0, col_copy, 1),
        (g < n_grp - 1, row_copy, 0),
        (g > 0, row_copy, 1),
    ]
    gets = [
        (g > 0, row_copy, 0),
        (g < n_grp - 1, row_copy, 1),
        (b > 0, col_copy, 0),
        (b < n_blk - 1, col_copy, 1),
    ]

    arrivals = [jnp.where(early, m, i) for m, i in [(1, 2), (0, 3), (3, 1), (2, 0)]]
    for i in arrivals:
        gather(i, 0)
    for r in range(prows):
        col_out[0, r : r + 1] = restricted[(r + 1) * pcols - 1 : (r + 1) * pcols]
        col_out[1, r : r + 1] = restricted[r * pcols : r * pcols + 1]
    row_out[0] = restricted[cells - pcols :]
    row_out[1] = restricted[:pcols]
    @pl.when(g < n_grp - 1)
    def _():
        pl.semaphore_wait(ready.at[PEERS], 1)

    for here, copy, side in sends:

        @pl.when(here)
        def _():
            copy(side).start()

    if paired:
        swap = early.astype(i32)
        gather_pair(swap)
        gather_pair(1 - swap)
    elif parts == 2:
        for i in arrivals:
            gather(i, 1)

    for here, copy, side in gets:

        @pl.when(here)
        def _():
            copy(side).wait_recv()

    col = lax.rem(lax.broadcasted_iota(i32, (cells, chunk), 0), pcols)
    for c in range(channels // chunk):
        at = slice(c * chunk, (c + 1) * chunk)
        own = restricted[:, at]

        def widened(side):
            return jnp.broadcast_to(
                col_halo[side, :, at][:, None, :], (prows, pcols, chunk)
            ).reshape(cells, chunk)

        up = jnp.concatenate([row_halo[0, :, at], own[: cells - pcols]], axis=0)
        down = jnp.concatenate([own[pcols:], row_halo[1, :, at]], axis=0)
        left = jnp.where(col == 0, widened(0), pltpu.roll(own, 1, 0))
        right = jnp.where(col == pcols - 1, widened(1), pltpu.roll(own, cells - 1, 0))
        beside = down + up + right + left
        out_ref[:, at] = own + theta_wide[...] * (beside - 4.0 * own)

    for i in range(PEERS):
        number_copy(i).wait_send()
        for part in range(parts):
            piece_copy(i, part).wait_send()
    for here, copy, side in sends:

        @pl.when(here)
        def _():
            copy(side).wait_send()


def body(n_grp, n_blk, child_field, child_weight, child_slot, send_list, theta):
    children, channels = child_field.shape
    prows, pcols = theta.shape
    cells = prows * pcols
    cap = send_list.shape[1] // (PEERS + 1)
    rim = 2 * (prows + pcols) - 4
    head = min(cap, -(-rim // SUB) * SUB)
    groups = children // LANES
    f32, bf16, i32 = jnp.float32, jnp.bfloat16, jnp.int32
    dma = pltpu.SemaphoreType.DMA
    out = pl.pallas_call(
        functools.partial(kernel, n_grp, n_blk, prows, pcols, cap, head),
        out_shape=pltpu.VMEM((cells, channels), f32),
        in_specs=[pl.BlockSpec(memory_space=pltpu.HBM)] * 5,
        out_specs=pl.BlockSpec(memory_space=pltpu.VMEM),
        scratch_shapes=[
            pltpu.VMEM((children, channels), bf16),
            pltpu.VMEM((groups, LANES), bf16),
            pltpu.VMEM((groups, LANES), i32),
            pltpu.VMEM(send_list.shape, i32),
            pltpu.VMEM((prows, pcols), f32),
            pltpu.VMEM((PEERS, cap, channels), f32),
            pltpu.VMEM((PEERS, cap, channels), f32),
            pltpu.VMEM((PEERS, 1, cap), i32),
            pltpu.VMEM((PEERS, 1, cap), i32),
            pltpu.VMEM((PEERS + 1, cap, LANES), i32),
            pltpu.VMEM((2, cap, children), bf16),
            pltpu.VMEM((PEERS + 3, cells, 2 * cap), bf16),
            pltpu.VMEM((cells, channels), f32),
            pltpu.VMEM((cells, LANES), f32),
            pltpu.VMEM((2, pcols, channels), f32),
            pltpu.VMEM((2, prows, channels), f32),
            pltpu.VMEM((2, pcols, channels), f32),
            pltpu.VMEM((2, prows, channels), f32),
            dma((4 + channels // LANES,)),
            dma((PEERS,)),
            dma((PEERS,)),
            dma((PEERS, 2)),
            dma((PEERS, 2)),
            dma((4,)),
            dma((4,)),
            pltpu.SemaphoreType.REGULAR((PEERS + 1,)),
        ],
        compiler_params=pltpu.CompilerParams(
            collective_id=0, has_side_effects=True, vmem_limit_bytes=32 * 1024 * 1024
        ),
        name="nest_feedback",
    )(
        *[
            pltpu.with_memory_space_constraint(x, pltpu.HBM)
            for x in (
                child_field,
                child_weight.reshape(groups, LANES),
                child_slot.reshape(groups, LANES),
                send_list,
                theta,
            )
        ]
    )
    return out.reshape(prows, pcols, channels)


def solution(mesh):
    return jax.shard_map(
        functools.partial(body, mesh.shape["grp"], mesh.shape["blk"]),
        mesh=mesh,
        in_specs=(
            P(("grp", "blk"), None),
            P(("grp", "blk")),
            P(("grp", "blk")),
            P(("grp", "blk"), None),
            P("grp", "blk"),
        ),
        out_specs=P("grp", "blk", None),
        check_vma=False,
    )
```

```python
import functools

import jax
import jax.numpy as jnp
from jax import lax
from jax.experimental import pallas as pl
from jax.experimental.pallas import tpu as pltpu
from jax.sharding import PartitionSpec as P

HALF = 2
PEERS = 2 * HALF
LANES = 128
SUB = 16
MESH = pl.DeviceIdType.MESH


def kernel(
    n_grp,
    n_blk,
    prows,
    pcols,
    cap,
    head,
    field_hbm,
    weight_hbm,
    slot_hbm,
    list_hbm,
    theta_hbm,
    out_ref,
    field,
    weight,
    slot,
    lists,
    theta,
    pieces,
    arrived,
    ordered,
    numbers,
    wanted,
    weighted,
    selector,
    restricted,
    theta_wide,
    row_out,
    col_out,
    row_halo,
    col_halo,
    in_sem,
    num_send,
    num_recv,
    piece_send,
    piece_recv,
    halo_send,
    halo_recv,
    ready,
):
    g = lax.axis_index("grp")
    b = lax.axis_index("blk")
    cells = prows * pcols
    children, channels = field.shape
    chunk = LANES
    parts = 2 if head < cap else 1
    f32, bf16, i32 = jnp.float32, jnp.bfloat16, jnp.int32
    early = b < HALF
    late = b >= n_blk - HALF

    def offset(i):
        if isinstance(i, int):
            return i - HALF + (i >= HALF)
        return i - HALF + (i >= HALF).astype(i32)

    def peer(i):
        return (g, lax.rem(b + offset(i) + n_blk, n_blk))

    turn = jnp.where(b == 0, 2, 0) + jnp.where(b == 1, 1, 0)
    turn = turn + jnp.where(b == n_blk - 2, 3, 0) + jnp.where(b == n_blk - 1, 2, 0)

    def nth(j):
        i = lax.rem(turn + j, PEERS)
        alt = [HALF, 0, HALF + 1, 1][j]
        return jnp.where((b == n_blk - 1) & (lax.rem(g, 2) == 1), alt, i)

    def above(i):
        return lax.rem(b + offset(i) + n_blk, n_blk) > b

    small = [
        pltpu.make_async_copy(src, dst, in_sem.at[i])
        for i, (src, dst) in enumerate(
            [(list_hbm, lists), (slot_hbm, slot), (weight_hbm, weight), (theta_hbm, theta)]
        )
    ]
    large = [
        pltpu.make_async_copy(
            field_hbm.at[:, pl.ds(q * chunk, chunk)],
            field.at[:, pl.ds(q * chunk, chunk)],
            in_sem.at[len(small) + q],
        )
        for q in range(channels // chunk)
    ]
    for load in [*small[:3], *large, small[3]]:
        load.start()

    barrier = pltpu.get_barrier_semaphore()
    greeted = (g > 0).astype(i32)
    for i in range(PEERS):

        @pl.when(above(i))
        def _():
            pl.semaphore_signal(barrier, inc=1, device_id=peer(i), device_id_type=MESH)

        greeted += 1 - above(i).astype(i32)

    @pl.when(g < n_grp - 1)
    def _():
        pl.semaphore_signal(barrier, inc=1, device_id=(g + 1, b), device_id_type=MESH)

    @pl.when(g == 0)
    def _():
        row_halo[0] = jnp.zeros_like(row_halo[0])

    @pl.when(g == n_grp - 1)
    def _():
        row_halo[1] = jnp.zeros_like(row_halo[1])

    @pl.when(b == 0)
    def _():
        col_halo[0] = jnp.zeros_like(col_halo[0])

    @pl.when(b == n_blk - 1)
    def _():
        col_halo[1] = jnp.zeros_like(col_halo[1])

    small[0].wait()
    lane = lax.broadcasted_iota(i32, (cap, cap), 1)
    sub = lax.broadcasted_iota(i32, (cap, cap), 0)
    owned = [0, 1, 3, 4]
    table = jnp.concatenate(
        [lists[:, k * cap : (k + 1) * cap] for k in owned]
        + [jnp.full((SUB - PEERS, cap), -1, i32)],
        axis=0,
    )
    place = lax.rem(table, pcols)
    rim = (table < pcols) | (table >= cells - pcols) | (place == 0) | (place == pcols - 1)
    rim = rim & (table >= 0)
    ones = jnp.where(rim, 1.0, 0.0)
    before = jnp.dot(
        ones.astype(bf16), jnp.where(sub < lane, 1.0, 0.0).astype(bf16), preferred_element_type=f32
    )
    count = jnp.sum(ones, axis=1, keepdims=True)
    own_lane = lax.broadcasted_iota(i32, (SUB, cap), 1).astype(f32)
    position = jnp.where(rim, before, count + own_lane - before).astype(i32)
    high, low = table[:8] >> 7, table[:8] & 127
    halves = jnp.concatenate([high, low], axis=0).astype(f32).astype(bf16)
    for i in range(PEERS):
        goes = position[i : i + 1, :] == sub
        source = jnp.sum(jnp.where(goes, lane, 0), axis=1, keepdims=True)
        wanted[i] = jnp.broadcast_to(source + owned[i] * cap, (cap, LANES))
        moved = lax.dot_general(
            halves,
            jnp.where(goes, 1.0, 0.0).astype(bf16),
            (((1,), (1,)), ((), ())),
            preferred_element_type=f32,
        ).astype(i32)
        ordered[i] = moved[i : i + 1, :] * 128 + moved[8 + i : 9 + i, :]
    wanted[PEERS] = sub + HALF * cap

    small[1].wait()
    small[2].wait()
    slots = slot[...]
    weights = weight[...].astype(f32)

    def weigh(i, at):
        ids = wanted[i]
        for j in range(children // LANES):
            hit = jnp.where(ids == slots[j : j + 1, :], weights[j : j + 1, :], 0.0)
            weighted[at, :, j * LANES : (j + 1) * LANES] = hit.astype(bf16)

    def number_copy(i):
        return pltpu.make_async_remote_copy(
            src_ref=ordered.at[i],
            dst_ref=numbers.at[i],
            send_sem=num_send.at[i],
            recv_sem=num_recv.at[i],
            device_id=peer(i),
            device_id_type=MESH,
        )

    spans = [pl.ds(0, head), pl.ds(head, cap - head)]

    def piece_copy(i, part):
        return pltpu.make_async_remote_copy(
            src_ref=pieces.at[i, spans[part]],
            dst_ref=arrived.at[i, spans[part]],
            send_sem=piece_send.at[i, part],
            recv_sem=piece_recv.at[i, part],
            device_id=peer(i),
            device_id_type=MESH,
        )

    def first_copy(i, start):
        at = pl.ds(start, chunk)
        return pltpu.make_async_remote_copy(
            src_ref=pieces.at[i, spans[0], at],
            dst_ref=arrived.at[i, spans[0], at],
            send_sem=piece_send.at[i, 0],
            recv_sem=piece_recv.at[i, 0],
            device_id=peer(i),
            device_id_type=MESH,
        )

    def tail(j):
        if parts == 2:
            piece_copy(nth(j), 1).start()

    @pl.when(greeted > 0)
    def _():
        pl.semaphore_wait(barrier, greeted)

    for q in range(PEERS):

        @pl.when(~above(q))
        def _():
            pl.semaphore_signal(
                ready.at[q], inc=1, device_id=peer(q), device_id_type=MESH
            )

    @pl.when(g > 0)
    def _():
        pl.semaphore_signal(
            ready.at[PEERS], inc=1, device_id=(g - 1, b), device_id_type=MESH
        )

    weigh(nth(0), 0)
    for j in range(PEERS):
        i = nth(j)
        if j > 0:
            weigh(i, j % 2)
            pieces[i] = jnp.dot(weighted[j % 2], field[...], preferred_element_type=f32)

        @pl.when(above(i))
        def _():
            pl.semaphore_wait(ready.at[PEERS - 1 - i], 1)

        number_copy(i).start()
        if j > 0:
            piece_copy(i, 0).start()
        else:
            for q, load in enumerate(large):
                load.wait()
                at = slice(q * chunk, (q + 1) * chunk)
                pieces[i, :, at] = jnp.dot(weighted[0], field[:, at], preferred_element_type=f32)
                first_copy(i, q * chunk).start()
        if j == 1:

            @pl.when((b == n_blk - 1) & (g == 0))
            def _():
                tail(0)

    last = (b == n_blk - 1) & (lax.rem(g, 2) == 1)

    @pl.when(~((b == n_blk - 1) & (g == 0)))
    def _():
        tail(0)

    @pl.when(last)
    def _():
        tail(2)

    tail(1)

    @pl.when(~last)
    def _():
        tail(2)

    tail(3)

    def select(i, entries):
        hit = lax.broadcasted_iota(i32, (cells, cap), 0) == entries
        hit = jnp.where(hit, 1.0, 0.0).astype(bf16)
        selector[i] = jnp.concatenate([hit, hit], axis=1)

    def split(piece):
        top = piece.astype(bf16)
        return top, (piece - top.astype(f32)).astype(bf16)

    def spread(i, rows_of):
        return jnp.dot(selector[i], jnp.concatenate(rows_of, axis=0), preferred_element_type=f32)

    select(PEERS, lists[:, HALF * cap : (HALF + 1) * cap])
    weigh(PEERS, 0)
    made = jnp.dot(weighted[0], field[...], preferred_element_type=f32)
    restricted[...] = spread(PEERS, split(made))

    small[3].wait()
    diagonal = lax.broadcasted_iota(i32, (pcols, pcols), 0) == lax.broadcasted_iota(
        i32, (pcols, pcols), 1
    )
    for r in range(prows):
        column = jnp.sum(jnp.where(diagonal, theta[r : r + 1, :], 0.0), axis=1, keepdims=True)
        theta_wide[r * pcols : (r + 1) * pcols, :] = jnp.broadcast_to(column, (pcols, chunk))

    for i in range(PEERS):
        number_copy(i).wait_recv()
        select(i, numbers[i])

    rest = cap - head
    paired = parts == 2 and rest <= head
    if paired:
        lane8 = lax.broadcasted_iota(i32, (8, cap), 1)
        for p in range(2):
            first = jnp.broadcast_to(numbers[2 - p], (8, cap))
            second = pltpu.roll(jnp.broadcast_to(numbers[3 - 3 * p], (8, cap)), cap - rest, 1)
            both = jnp.where(lane8 >= head, first, jnp.where(lane8 >= head - rest, second, -1))
            select(PEERS + 1 + p, both[:1])

    def gather_pair(p):
        rows_of = [[], []]
        for i in (3 - 3 * p, 2 - p):
            piece_copy(i, 1).wait_recv()
            for side, value in enumerate(split(arrived[i, spans[1]])):
                rows_of[side].append(value)
        if head > rest:
            gap = [jnp.zeros((head - rest, channels), bf16)]
        else:
            gap = []
        restricted[...] += spread(PEERS + 1 + p, [*gap, *rows_of[0], *gap, *rows_of[1]])

    blank = [jnp.zeros((head, channels), bf16), jnp.zeros((cap - head, channels), bf16)]

    def gather(i, part):
        piece_copy(i, part).wait_recv()
        top, rest = split(arrived[i, spans[part]])
        if parts == 1:
            rows_of = [top, rest]
        elif part == 0:
            rows_of = [top, blank[1], rest, blank[1]]
        else:
            rows_of = [blank[0], top, blank[0], rest]
        restricted[...] += spread(i, rows_of)

    def row_copy(side):
        return pltpu.make_async_remote_copy(
            src_ref=row_out.at[side],
            dst_ref=row_halo.at[side],
            send_sem=halo_send.at[side],
            recv_sem=halo_recv.at[side],
            device_id=(g - 1 if side else g + 1, b),
            device_id_type=MESH,
        )

    def col_copy(side):
        return pltpu.make_async_remote_copy(
            src_ref=col_out.at[side],
            dst_ref=col_halo.at[side],
            send_sem=halo_send.at[2 + side],
            recv_sem=halo_recv.at[2 + side],
            device_id=(g, b - 1 if side else b + 1),
            device_id_type=MESH,
        )

    sends = [
        (b < n_blk - 1, col_copy, 0),
        (b > 0, col_copy, 1),
        (g < n_grp - 1, row_copy, 0),
        (g > 0, row_copy, 1),
    ]
    gets = [
        (g > 0, row_copy, 0),
        (g < n_grp - 1, row_copy, 1),
        (b > 0, col_copy, 0),
        (b < n_blk - 1, col_copy, 1),
    ]

    arrivals = [2, 3, 1, 0]
    for i in arrivals:
        gather(i, 0)
    for r in range(prows):
        col_out[0, r : r + 1] = restricted[(r + 1) * pcols - 1 : (r + 1) * pcols]
        col_out[1, r : r + 1] = restricted[r * pcols : r * pcols + 1]
    row_out[0] = restricted[cells - pcols :]
    row_out[1] = restricted[:pcols]
    @pl.when(g < n_grp - 1)
    def _():
        pl.semaphore_wait(ready.at[PEERS], 1)

    for here, copy, side in sends:

        @pl.when(here)
        def _():
            copy(side).start()

    if paired:
        swap = early.astype(i32)
        gather_pair(swap)
        gather_pair(1 - swap)
    elif parts == 2:
        for i in arrivals:
            gather(i, 1)

    for here, copy, side in gets:

        @pl.when(here)
        def _():
            copy(side).wait_recv()

    col = lax.rem(lax.broadcasted_iota(i32, (cells, chunk), 0), pcols)
    for c in range(channels // chunk):
        at = slice(c * chunk, (c + 1) * chunk)
        own = restricted[:, at]

        def widened(side):
            return jnp.broadcast_to(
                col_halo[side, :, at][:, None, :], (prows, pcols, chunk)
            ).reshape(cells, chunk)

        up = jnp.concatenate([row_halo[0, :, at], own[: cells - pcols]], axis=0)
        down = jnp.concatenate([own[pcols:], row_halo[1, :, at]], axis=0)
        left = jnp.where(col == 0, widened(0), pltpu.roll(own, 1, 0))
        right = jnp.where(col == pcols - 1, widened(1), pltpu.roll(own, cells - 1, 0))
        beside = down + up + right + left
        out_ref[:, at] = own + theta_wide[...] * (beside - 4.0 * own)

    for i in range(PEERS):
        number_copy(i).wait_send()
        for part in range(parts):
            piece_copy(i, part).wait_send()
    for here, copy, side in sends:

        @pl.when(here)
        def _():
            copy(side).wait_send()


def body(n_grp, n_blk, child_field, child_weight, child_slot, send_list, theta):
    children, channels = child_field.shape
    prows, pcols = theta.shape
    cells = prows * pcols
    cap = send_list.shape[1] // (PEERS + 1)
    rim = 2 * (prows + pcols) - 4
    head = min(cap, -(-rim // SUB) * SUB)
    groups = children // LANES
    f32, bf16, i32 = jnp.float32, jnp.bfloat16, jnp.int32
    dma = pltpu.SemaphoreType.DMA
    out = pl.pallas_call(
        functools.partial(kernel, n_grp, n_blk, prows, pcols, cap, head),
        out_shape=pltpu.VMEM((cells, channels), f32),
        in_specs=[pl.BlockSpec(memory_space=pltpu.HBM)] * 5,
        out_specs=pl.BlockSpec(memory_space=pltpu.VMEM),
        scratch_shapes=[
            pltpu.VMEM((children, channels), bf16),
            pltpu.VMEM((groups, LANES), bf16),
            pltpu.VMEM((groups, LANES), i32),
            pltpu.VMEM(send_list.shape, i32),
            pltpu.VMEM((prows, pcols), f32),
            pltpu.VMEM((PEERS, cap, channels), f32),
            pltpu.VMEM((PEERS, cap, channels), f32),
            pltpu.VMEM((PEERS, 1, cap), i32),
            pltpu.VMEM((PEERS, 1, cap), i32),
            pltpu.VMEM((PEERS + 1, cap, LANES), i32),
            pltpu.VMEM((2, cap, children), bf16),
            pltpu.VMEM((PEERS + 3, cells, 2 * cap), bf16),
            pltpu.VMEM((cells, channels), f32),
            pltpu.VMEM((cells, LANES), f32),
            pltpu.VMEM((2, pcols, channels), f32),
            pltpu.VMEM((2, prows, channels), f32),
            pltpu.VMEM((2, pcols, channels), f32),
            pltpu.VMEM((2, prows, channels), f32),
            dma((4 + channels // LANES,)),
            dma((PEERS,)),
            dma((PEERS,)),
            dma((PEERS, 2)),
            dma((PEERS, 2)),
            dma((4,)),
            dma((4,)),
            pltpu.SemaphoreType.REGULAR((PEERS + 1,)),
        ],
        compiler_params=pltpu.CompilerParams(
            collective_id=0, has_side_effects=True, vmem_limit_bytes=32 * 1024 * 1024
        ),
        name="nest_feedback",
    )(
        *[
            pltpu.with_memory_space_constraint(x, pltpu.HBM)
            for x in (
                child_field,
                child_weight.reshape(groups, LANES),
                child_slot.reshape(groups, LANES),
                send_list,
                theta,
            )
        ]
    )
    return out.reshape(prows, pcols, channels)


def solution(mesh):
    return jax.shard_map(
        functools.partial(body, mesh.shape["grp"], mesh.shape["blk"]),
        mesh=mesh,
        in_specs=(
            P(("grp", "blk"), None),
            P(("grp", "blk")),
            P(("grp", "blk")),
            P(("grp", "blk"), None),
            P("grp", "blk"),
        ),
        out_specs=P("grp", "blk", None),
        check_vma=False,
    )
```

```python
import functools

import jax
import jax.numpy as jnp
from jax import lax
from jax.experimental import pallas as pl
from jax.experimental.pallas import tpu as pltpu
from jax.sharding import PartitionSpec as P

HALF = 2
PEERS = 2 * HALF
LANES = 128
SUB = 16
MESH = pl.DeviceIdType.MESH


def kernel(
    n_grp,
    n_blk,
    prows,
    pcols,
    cap,
    head,
    field_hbm,
    weight_hbm,
    slot_hbm,
    list_hbm,
    theta_hbm,
    out_ref,
    field,
    weight,
    slot,
    lists,
    theta,
    pieces,
    arrived,
    ordered,
    numbers,
    wanted,
    weighted,
    selector,
    restricted,
    theta_wide,
    row_out,
    col_out,
    row_halo,
    col_halo,
    in_sem,
    num_send,
    num_recv,
    piece_send,
    piece_recv,
    halo_send,
    halo_recv,
    ready,
):
    g = lax.axis_index("grp")
    b = lax.axis_index("blk")
    cells = prows * pcols
    children, channels = field.shape
    chunk = LANES
    parts = 2 if head < cap else 1
    f32, bf16, i32 = jnp.float32, jnp.bfloat16, jnp.int32
    early = b < HALF
    late = b >= n_blk - HALF

    def offset(i):
        if isinstance(i, int):
            return i - HALF + (i >= HALF)
        return i - HALF + (i >= HALF).astype(i32)

    def peer(i):
        return (g, lax.rem(b + offset(i) + n_blk, n_blk))

    turn = jnp.where(b == 0, 2, 0) + jnp.where(b == 1, 1, 0)
    turn = turn + jnp.where(b == n_blk - 2, 3, 0) + jnp.where(b == n_blk - 1, 2, 0)

    def nth(j):
        i = lax.rem(turn + j, PEERS)
        alt = [HALF, 0, HALF + 1, 1][j]
        return jnp.where((b == n_blk - 1) & (lax.rem(g, 2) == 1), alt, i)

    def above(i):
        return lax.rem(b + offset(i) + n_blk, n_blk) > b

    small = [
        pltpu.make_async_copy(src, dst, in_sem.at[i])
        for i, (src, dst) in enumerate(
            [(list_hbm, lists), (slot_hbm, slot), (weight_hbm, weight), (theta_hbm, theta)]
        )
    ]
    large = [
        pltpu.make_async_copy(
            field_hbm.at[:, pl.ds(q * chunk, chunk)],
            field.at[:, pl.ds(q * chunk, chunk)],
            in_sem.at[len(small) + q],
        )
        for q in range(channels // chunk)
    ]
    for load in [*small[:3], *large, small[3]]:
        load.start()

    barrier = pltpu.get_barrier_semaphore()
    greeted = (g > 0).astype(i32)
    for i in range(PEERS):

        @pl.when(above(i))
        def _():
            pl.semaphore_signal(barrier, inc=1, device_id=peer(i), device_id_type=MESH)

        greeted += 1 - above(i).astype(i32)

    @pl.when(g < n_grp - 1)
    def _():
        pl.semaphore_signal(barrier, inc=1, device_id=(g + 1, b), device_id_type=MESH)

    @pl.when(g == 0)
    def _():
        row_halo[0] = jnp.zeros_like(row_halo[0])

    @pl.when(g == n_grp - 1)
    def _():
        row_halo[1] = jnp.zeros_like(row_halo[1])

    @pl.when(b == 0)
    def _():
        col_halo[0] = jnp.zeros_like(col_halo[0])

    @pl.when(b == n_blk - 1)
    def _():
        col_halo[1] = jnp.zeros_like(col_halo[1])

    small[0].wait()
    lane = lax.broadcasted_iota(i32, (cap, cap), 1)
    sub = lax.broadcasted_iota(i32, (cap, cap), 0)
    owned = [0, 1, 3, 4]
    table = jnp.concatenate(
        [lists[:, k * cap : (k + 1) * cap] for k in owned]
        + [jnp.full((SUB - PEERS, cap), -1, i32)],
        axis=0,
    )
    place = lax.rem(table, pcols)
    rim = (table < pcols) | (table >= cells - pcols) | (place == 0) | (place == pcols - 1)
    rim = rim & (table >= 0)
    ones = jnp.where(rim, 1.0, 0.0)
    before = jnp.dot(
        ones.astype(bf16), jnp.where(sub < lane, 1.0, 0.0).astype(bf16), preferred_element_type=f32
    )
    count = jnp.sum(ones, axis=1, keepdims=True)
    own_lane = lax.broadcasted_iota(i32, (SUB, cap), 1).astype(f32)
    position = jnp.where(rim, before, count + own_lane - before).astype(i32)
    high, low = table[:8] >> 7, table[:8] & 127
    halves = jnp.concatenate([high, low], axis=0).astype(f32).astype(bf16)
    for i in range(PEERS):
        goes = position[i : i + 1, :] == sub
        source = jnp.sum(jnp.where(goes, lane, 0), axis=1, keepdims=True)
        wanted[i] = jnp.broadcast_to(source + owned[i] * cap, (cap, LANES))
        moved = lax.dot_general(
            halves,
            jnp.where(goes, 1.0, 0.0).astype(bf16),
            (((1,), (1,)), ((), ())),
            preferred_element_type=f32,
        ).astype(i32)
        ordered[i] = moved[i : i + 1, :] * 128 + moved[8 + i : 9 + i, :]
    wanted[PEERS] = sub + HALF * cap

    small[1].wait()
    small[2].wait()
    slots = slot[...]
    weights = weight[...].astype(f32)

    def weigh(i, at):
        ids = wanted[i]
        for j in range(children // LANES):
            hit = jnp.where(ids == slots[j : j + 1, :], weights[j : j + 1, :], 0.0)
            weighted[at, :, j * LANES : (j + 1) * LANES] = hit.astype(bf16)

    def number_copy(i):
        return pltpu.make_async_remote_copy(
            src_ref=ordered.at[i],
            dst_ref=numbers.at[i],
            send_sem=num_send.at[i],
            recv_sem=num_recv.at[i],
            device_id=peer(i),
            device_id_type=MESH,
        )

    spans = [pl.ds(0, head), pl.ds(head, cap - head)]

    def piece_copy(i, part):
        return pltpu.make_async_remote_copy(
            src_ref=pieces.at[i, spans[part]],
            dst_ref=arrived.at[i, spans[part]],
            send_sem=piece_send.at[i, part],
            recv_sem=piece_recv.at[i, part],
            device_id=peer(i),
            device_id_type=MESH,
        )

    def first_copy(i, start):
        at = pl.ds(start, chunk)
        return pltpu.make_async_remote_copy(
            src_ref=pieces.at[i, spans[0], at],
            dst_ref=arrived.at[i, spans[0], at],
            send_sem=piece_send.at[i, 0],
            recv_sem=piece_recv.at[i, 0],
            device_id=peer(i),
            device_id_type=MESH,
        )

    def tail(j):
        if parts == 2:
            piece_copy(nth(j), 1).start()

    @pl.when(greeted > 0)
    def _():
        pl.semaphore_wait(barrier, greeted)

    for q in range(PEERS):

        @pl.when(~above(q))
        def _():
            pl.semaphore_signal(
                ready.at[q], inc=1, device_id=peer(q), device_id_type=MESH
            )

    @pl.when(g > 0)
    def _():
        pl.semaphore_signal(
            ready.at[PEERS], inc=1, device_id=(g - 1, b), device_id_type=MESH
        )

    weigh(nth(0), 0)
    for j in range(PEERS):
        i = nth(j)
        if j > 0:
            weigh(i, j % 2)
            pieces[i] = jnp.dot(weighted[j % 2], field[...], preferred_element_type=f32)

        @pl.when(above(i))
        def _():
            pl.semaphore_wait(ready.at[PEERS - 1 - i], 1)

        number_copy(i).start()
        if j > 0:
            piece_copy(i, 0).start()
        else:
            for q, load in enumerate(large):
                load.wait()
                at = slice(q * chunk, (q + 1) * chunk)
                pieces[i, :, at] = jnp.dot(weighted[0], field[:, at], preferred_element_type=f32)
                first_copy(i, q * chunk).start()
        if j == 1:

            @pl.when((b == n_blk - 1) & (g == 0))
            def _():
                tail(0)

    last = (b == n_blk - 1) & (lax.rem(g, 2) == 1)

    @pl.when(~((b == n_blk - 1) & (g == 0)))
    def _():
        tail(0)

    @pl.when(last)
    def _():
        tail(2)

    tail(1)

    @pl.when(~last)
    def _():
        tail(2)

    tail(3)

    def select(i, entries):
        hit = lax.broadcasted_iota(i32, (cells, cap), 0) == entries
        hit = jnp.where(hit, 1.0, 0.0).astype(bf16)
        selector[i] = jnp.concatenate([hit, hit], axis=1)

    def split(piece):
        top = piece.astype(bf16)
        return top, (piece - top.astype(f32)).astype(bf16)

    def spread(i, rows_of):
        return jnp.dot(selector[i], jnp.concatenate(rows_of, axis=0), preferred_element_type=f32)

    select(PEERS, lists[:, HALF * cap : (HALF + 1) * cap])
    weigh(PEERS, 0)
    made = jnp.dot(weighted[0], field[...], preferred_element_type=f32)
    restricted[...] = spread(PEERS, split(made))

    small[3].wait()
    diagonal = lax.broadcasted_iota(i32, (pcols, pcols), 0) == lax.broadcasted_iota(
        i32, (pcols, pcols), 1
    )
    for r in range(prows):
        column = jnp.sum(jnp.where(diagonal, theta[r : r + 1, :], 0.0), axis=1, keepdims=True)
        theta_wide[r * pcols : (r + 1) * pcols, :] = jnp.broadcast_to(column, (pcols, chunk))

    for i in range(PEERS):
        number_copy(i).wait_recv()
        select(i, numbers[i])

    rest = cap - head
    paired = parts == 2 and rest <= head
    if paired:
        lane8 = lax.broadcasted_iota(i32, (8, cap), 1)
        for p in range(2):
            first = jnp.broadcast_to(numbers[2 - p], (8, cap))
            second = pltpu.roll(jnp.broadcast_to(numbers[3 - 3 * p], (8, cap)), cap - rest, 1)
            both = jnp.where(lane8 >= head, first, jnp.where(lane8 >= head - rest, second, -1))
            select(PEERS + 1 + p, both[:1])

    def settle():
        for i in range(PEERS):
            number_copy(i).wait_send()
            piece_copy(i, 0).wait_send()

    def gather_pair(p):
        rows_of = [[], []]
        for i in (3 - 3 * p, 2 - p):
            piece_copy(i, 1).wait_recv()
            for side, value in enumerate(split(arrived[i, spans[1]])):
                rows_of[side].append(value)
        if head > rest:
            gap = [jnp.zeros((head - rest, channels), bf16)]
        else:
            gap = []
        return spread(PEERS + 1 + p, [*gap, *rows_of[0], *gap, *rows_of[1]])

    blank = [jnp.zeros((head, channels), bf16), jnp.zeros((cap - head, channels), bf16)]

    def gather(i, part):
        piece_copy(i, part).wait_recv()
        top, rest = split(arrived[i, spans[part]])
        if parts == 1:
            rows_of = [top, rest]
        elif part == 0:
            rows_of = [top, blank[1], rest, blank[1]]
        else:
            rows_of = [blank[0], top, blank[0], rest]
        restricted[...] += spread(i, rows_of)

    def row_copy(side):
        return pltpu.make_async_remote_copy(
            src_ref=row_out.at[side],
            dst_ref=row_halo.at[side],
            send_sem=halo_send.at[side],
            recv_sem=halo_recv.at[side],
            device_id=(g - 1 if side else g + 1, b),
            device_id_type=MESH,
        )

    def col_copy(side):
        return pltpu.make_async_remote_copy(
            src_ref=col_out.at[side],
            dst_ref=col_halo.at[side],
            send_sem=halo_send.at[2 + side],
            recv_sem=halo_recv.at[2 + side],
            device_id=(g, b - 1 if side else b + 1),
            device_id_type=MESH,
        )

    sends = [
        (b < n_blk - 1, col_copy, 0),
        (b > 0, col_copy, 1),
        (g < n_grp - 1, row_copy, 0),
        (g > 0, row_copy, 1),
    ]
    gets = [
        (g > 0, row_copy, 0),
        (g < n_grp - 1, row_copy, 1),
        (b > 0, col_copy, 0),
        (b < n_blk - 1, col_copy, 1),
    ]

    arrivals = [2, 3, 1, 0]
    for i in arrivals:
        gather(i, 0)
    for r in range(prows):
        col_out[0, r : r + 1] = restricted[(r + 1) * pcols - 1 : (r + 1) * pcols]
        col_out[1, r : r + 1] = restricted[r * pcols : r * pcols + 1]
    row_out[0] = restricted[cells - pcols :]
    row_out[1] = restricted[:pcols]
    @pl.when(g < n_grp - 1)
    def _():
        pl.semaphore_wait(ready.at[PEERS], 1)

    for here, copy, side in sends:

        @pl.when(here)
        def _():
            copy(side).start()

    if paired:
        swap = early.astype(i32)
        restricted[...] += gather_pair(swap)
        settle()
        total = restricted[...] + gather_pair(1 - swap)
    elif parts == 2:
        settle()
        for i in arrivals:
            gather(i, 1)
    else:
        settle()

    for here, copy, side in gets:

        @pl.when(here)
        def _():
            copy(side).wait_recv()

    col = lax.rem(lax.broadcasted_iota(i32, (cells, chunk), 0), pcols)
    for c in range(channels // chunk):
        at = slice(c * chunk, (c + 1) * chunk)
        own = total[:, at] if paired else restricted[:, at]

        def widened(side):
            return jnp.broadcast_to(
                col_halo[side, :, at][:, None, :], (prows, pcols, chunk)
            ).reshape(cells, chunk)

        up = jnp.concatenate([row_halo[0, :, at], own[: cells - pcols]], axis=0)
        down = jnp.concatenate([own[pcols:], row_halo[1, :, at]], axis=0)
        left = jnp.where(col == 0, widened(0), pltpu.roll(own, 1, 0))
        right = jnp.where(col == pcols - 1, widened(1), pltpu.roll(own, cells - 1, 0))
        beside = down + up + right + left
        out_ref[:, at] = own + theta_wide[...] * (beside - 4.0 * own)

    for i in range(PEERS):
        if parts == 2:
            piece_copy(i, 1).wait_send()
    for here, copy, side in sends:

        @pl.when(here)
        def _():
            copy(side).wait_send()


def body(n_grp, n_blk, child_field, child_weight, child_slot, send_list, theta):
    children, channels = child_field.shape
    prows, pcols = theta.shape
    cells = prows * pcols
    cap = send_list.shape[1] // (PEERS + 1)
    rim = 2 * (prows + pcols) - 4
    head = min(cap, -(-rim // SUB) * SUB)
    groups = children // LANES
    f32, bf16, i32 = jnp.float32, jnp.bfloat16, jnp.int32
    dma = pltpu.SemaphoreType.DMA
    out = pl.pallas_call(
        functools.partial(kernel, n_grp, n_blk, prows, pcols, cap, head),
        out_shape=pltpu.VMEM((cells, channels), f32),
        in_specs=[pl.BlockSpec(memory_space=pltpu.HBM)] * 5,
        out_specs=pl.BlockSpec(memory_space=pltpu.VMEM),
        scratch_shapes=[
            pltpu.VMEM((children, channels), bf16),
            pltpu.VMEM((groups, LANES), bf16),
            pltpu.VMEM((groups, LANES), i32),
            pltpu.VMEM(send_list.shape, i32),
            pltpu.VMEM((prows, pcols), f32),
            pltpu.VMEM((PEERS, cap, channels), f32),
            pltpu.VMEM((PEERS, cap, channels), f32),
            pltpu.VMEM((PEERS, 1, cap), i32),
            pltpu.VMEM((PEERS, 1, cap), i32),
            pltpu.VMEM((PEERS + 1, cap, LANES), i32),
            pltpu.VMEM((2, cap, children), bf16),
            pltpu.VMEM((PEERS + 3, cells, 2 * cap), bf16),
            pltpu.VMEM((cells, channels), f32),
            pltpu.VMEM((cells, LANES), f32),
            pltpu.VMEM((2, pcols, channels), f32),
            pltpu.VMEM((2, prows, channels), f32),
            pltpu.VMEM((2, pcols, channels), f32),
            pltpu.VMEM((2, prows, channels), f32),
            dma((4 + channels // LANES,)),
            dma((PEERS,)),
            dma((PEERS,)),
            dma((PEERS, 2)),
            dma((PEERS, 2)),
            dma((4,)),
            dma((4,)),
            pltpu.SemaphoreType.REGULAR((PEERS + 1,)),
        ],
        compiler_params=pltpu.CompilerParams(
            collective_id=0, has_side_effects=True, vmem_limit_bytes=32 * 1024 * 1024
        ),
        name="nest_feedback",
    )(
        *[
            pltpu.with_memory_space_constraint(x, pltpu.HBM)
            for x in (
                child_field,
                child_weight.reshape(groups, LANES),
                child_slot.reshape(groups, LANES),
                send_list,
                theta,
            )
        ]
    )
    return out.reshape(prows, pcols, channels)


def solution(mesh):
    return jax.shard_map(
        functools.partial(body, mesh.shape["grp"], mesh.shape["blk"]),
        mesh=mesh,
        in_specs=(
            P(("grp", "blk"), None),
            P(("grp", "blk")),
            P(("grp", "blk")),
            P(("grp", "blk"), None),
            P("grp", "blk"),
        ),
        out_specs=P("grp", "blk", None),
        check_vma=False,
    )
```

```python
import functools

import jax
import jax.numpy as jnp
from jax import lax
from jax.experimental import pallas as pl
from jax.experimental.pallas import tpu as pltpu
from jax.sharding import PartitionSpec as P

HALF = 2
PEERS = 2 * HALF
LANES = 128
SUB = 16
MESH = pl.DeviceIdType.MESH


def kernel(
    n_grp,
    n_blk,
    prows,
    pcols,
    cap,
    head,
    field_hbm,
    weight_hbm,
    slot_hbm,
    list_hbm,
    theta_hbm,
    out_ref,
    field,
    weight,
    slot,
    lists,
    theta,
    pieces,
    arrived,
    ordered,
    numbers,
    wanted,
    weighted,
    selector,
    restricted,
    theta_wide,
    row_out,
    col_out,
    row_halo,
    col_halo,
    in_sem,
    num_send,
    num_recv,
    piece_send,
    piece_recv,
    halo_send,
    halo_recv,
    ready,
):
    g = lax.axis_index("grp")
    b = lax.axis_index("blk")
    cells = prows * pcols
    children, channels = field.shape
    chunk = LANES
    parts = 2 if head < cap else 1
    f32, bf16, i32 = jnp.float32, jnp.bfloat16, jnp.int32
    early = b < HALF
    late = b >= n_blk - HALF

    def offset(i):
        if isinstance(i, int):
            return i - HALF + (i >= HALF)
        return i - HALF + (i >= HALF).astype(i32)

    def peer(i):
        return (g, lax.rem(b + offset(i) + n_blk, n_blk))

    turn = jnp.where(b == 0, 2, 0) + jnp.where(b == 1, 1, 0)
    turn = turn + jnp.where(b == n_blk - 2, 3, 0) + jnp.where(b == n_blk - 1, 2, 0)

    def nth(j):
        i = lax.rem(turn + j, PEERS)
        alt = [0, HALF, HALF + 1, 1][j]
        return jnp.where((b == n_blk - 1) & (lax.rem(g, 2) == 1), alt, i)

    def above(i):
        return lax.rem(b + offset(i) + n_blk, n_blk) > b

    small = [
        pltpu.make_async_copy(src, dst, in_sem.at[i])
        for i, (src, dst) in enumerate(
            [(list_hbm, lists), (slot_hbm, slot), (weight_hbm, weight), (theta_hbm, theta)]
        )
    ]
    large = [
        pltpu.make_async_copy(
            field_hbm.at[:, pl.ds(q * chunk, chunk)],
            field.at[:, pl.ds(q * chunk, chunk)],
            in_sem.at[len(small) + q],
        )
        for q in range(channels // chunk)
    ]
    for load in [*small[:3], *large, small[3]]:
        load.start()

    barrier = pltpu.get_barrier_semaphore()
    greeted = (g > 0).astype(i32)
    for i in range(PEERS):

        @pl.when(above(i))
        def _():
            pl.semaphore_signal(barrier, inc=1, device_id=peer(i), device_id_type=MESH)

        greeted += 1 - above(i).astype(i32)

    @pl.when(g < n_grp - 1)
    def _():
        pl.semaphore_signal(barrier, inc=1, device_id=(g + 1, b), device_id_type=MESH)

    @pl.when(g == 0)
    def _():
        row_halo[0] = jnp.zeros_like(row_halo[0])

    @pl.when(g == n_grp - 1)
    def _():
        row_halo[1] = jnp.zeros_like(row_halo[1])

    @pl.when(b == 0)
    def _():
        col_halo[0] = jnp.zeros_like(col_halo[0])

    @pl.when(b == n_blk - 1)
    def _():
        col_halo[1] = jnp.zeros_like(col_halo[1])

    small[0].wait()
    lane = lax.broadcasted_iota(i32, (cap, cap), 1)
    sub = lax.broadcasted_iota(i32, (cap, cap), 0)
    owned = [0, 1, 3, 4]
    table = jnp.concatenate(
        [lists[:, k * cap : (k + 1) * cap] for k in owned]
        + [jnp.full((SUB - PEERS, cap), -1, i32)],
        axis=0,
    )
    place = lax.rem(table, pcols)
    rim = (table < pcols) | (table >= cells - pcols) | (place == 0) | (place == pcols - 1)
    rim = rim & (table >= 0)
    ones = jnp.where(rim, 1.0, 0.0)
    before = jnp.dot(
        ones.astype(bf16), jnp.where(sub < lane, 1.0, 0.0).astype(bf16), preferred_element_type=f32
    )
    count = jnp.sum(ones, axis=1, keepdims=True)
    own_lane = lax.broadcasted_iota(i32, (SUB, cap), 1).astype(f32)
    position = jnp.where(rim, before, count + own_lane - before).astype(i32)
    high, low = table[:8] >> 7, table[:8] & 127
    halves = jnp.concatenate([high, low], axis=0).astype(f32).astype(bf16)
    for i in range(PEERS):
        goes = position[i : i + 1, :] == sub
        source = jnp.sum(jnp.where(goes, lane, 0), axis=1, keepdims=True)
        wanted[i] = jnp.broadcast_to(source + owned[i] * cap, (cap, LANES))
        moved = lax.dot_general(
            halves,
            jnp.where(goes, 1.0, 0.0).astype(bf16),
            (((1,), (1,)), ((), ())),
            preferred_element_type=f32,
        ).astype(i32)
        ordered[i] = moved[i : i + 1, :] * 128 + moved[8 + i : 9 + i, :]
    wanted[PEERS] = sub + HALF * cap

    small[1].wait()
    small[2].wait()
    slots = slot[...]
    weights = weight[...].astype(f32)

    def weigh(i, at):
        ids = wanted[i]
        for j in range(children // LANES):
            hit = jnp.where(ids == slots[j : j + 1, :], weights[j : j + 1, :], 0.0)
            weighted[at, :, j * LANES : (j + 1) * LANES] = hit.astype(bf16)

    def number_copy(i):
        return pltpu.make_async_remote_copy(
            src_ref=ordered.at[i],
            dst_ref=numbers.at[i],
            send_sem=num_send.at[i],
            recv_sem=num_recv.at[i],
            device_id=peer(i),
            device_id_type=MESH,
        )

    spans = [pl.ds(0, head), pl.ds(head, cap - head)]

    def piece_copy(i, part):
        return pltpu.make_async_remote_copy(
            src_ref=pieces.at[i, spans[part]],
            dst_ref=arrived.at[i, spans[part]],
            send_sem=piece_send.at[i, part],
            recv_sem=piece_recv.at[i, part],
            device_id=peer(i),
            device_id_type=MESH,
        )

    def first_copy(i, start):
        at = pl.ds(start, chunk)
        return pltpu.make_async_remote_copy(
            src_ref=pieces.at[i, spans[0], at],
            dst_ref=arrived.at[i, spans[0], at],
            send_sem=piece_send.at[i, 0],
            recv_sem=piece_recv.at[i, 0],
            device_id=peer(i),
            device_id_type=MESH,
        )

    def tail(j):
        if parts == 2:
            piece_copy(nth(j), 1).start()

    @pl.when(greeted > 0)
    def _():
        pl.semaphore_wait(barrier, greeted)

    for q in range(PEERS):

        @pl.when(~above(q))
        def _():
            pl.semaphore_signal(
                ready.at[q], inc=1, device_id=peer(q), device_id_type=MESH
            )

    @pl.when(g > 0)
    def _():
        pl.semaphore_signal(
            ready.at[PEERS], inc=1, device_id=(g - 1, b), device_id_type=MESH
        )

    weigh(nth(0), 0)
    for j in range(PEERS):
        i = nth(j)
        if j > 0:
            weigh(i, j % 2)
            pieces[i] = jnp.dot(weighted[j % 2], field[...], preferred_element_type=f32)

        @pl.when(above(i))
        def _():
            pl.semaphore_wait(ready.at[PEERS - 1 - i], 1)

        number_copy(i).start()
        if j > 0:
            piece_copy(i, 0).start()
        else:
            for q, load in enumerate(large):
                load.wait()
                at = slice(q * chunk, (q + 1) * chunk)
                pieces[i, :, at] = jnp.dot(weighted[0], field[:, at], preferred_element_type=f32)
                first_copy(i, q * chunk).start()
        if j == 1:

            @pl.when((b == n_blk - 1) & (g == 0))
            def _():
                tail(0)

    last = (b == n_blk - 1) & (lax.rem(g, 2) == 1)

    @pl.when(~((b == n_blk - 1) & (g == 0)) & ~last)
    def _():
        tail(0)

    tail(1)
    tail(2)

    @pl.when(last)
    def _():
        tail(0)

    tail(3)

    def select(i, entries):
        hit = lax.broadcasted_iota(i32, (cells, cap), 0) == entries
        hit = jnp.where(hit, 1.0, 0.0).astype(bf16)
        selector[i] = jnp.concatenate([hit, hit], axis=1)

    def split(piece):
        top = piece.astype(bf16)
        return top, (piece - top.astype(f32)).astype(bf16)

    def spread(i, rows_of):
        return jnp.dot(selector[i], jnp.concatenate(rows_of, axis=0), preferred_element_type=f32)

    select(PEERS, lists[:, HALF * cap : (HALF + 1) * cap])
    weigh(PEERS, 0)
    made = jnp.dot(weighted[0], field[...], preferred_element_type=f32)
    restricted[...] = spread(PEERS, split(made))

    small[3].wait()
    diagonal = lax.broadcasted_iota(i32, (pcols, pcols), 0) == lax.broadcasted_iota(
        i32, (pcols, pcols), 1
    )
    for r in range(prows):
        column = jnp.sum(jnp.where(diagonal, theta[r : r + 1, :], 0.0), axis=1, keepdims=True)
        theta_wide[r * pcols : (r + 1) * pcols, :] = jnp.broadcast_to(column, (pcols, chunk))

    for i in range(PEERS):
        number_copy(i).wait_recv()
        select(i, numbers[i])

    rest = cap - head
    paired = parts == 2 and rest <= head
    if paired:
        lane8 = lax.broadcasted_iota(i32, (8, cap), 1)
        for p in range(2):
            first = jnp.broadcast_to(numbers[2 - p], (8, cap))
            second = pltpu.roll(jnp.broadcast_to(numbers[3 - 3 * p], (8, cap)), cap - rest, 1)
            both = jnp.where(lane8 >= head, first, jnp.where(lane8 >= head - rest, second, -1))
            select(PEERS + 1 + p, both[:1])

    def settle():
        for i in range(PEERS):
            number_copy(i).wait_send()
            piece_copy(i, 0).wait_send()

    def gather_pair(p):
        rows_of = [[], []]
        for i in (3 - 3 * p, 2 - p):
            piece_copy(i, 1).wait_recv()
            for side, value in enumerate(split(arrived[i, spans[1]])):
                rows_of[side].append(value)
        if head > rest:
            gap = [jnp.zeros((head - rest, channels), bf16)]
        else:
            gap = []
        return spread(PEERS + 1 + p, [*gap, *rows_of[0], *gap, *rows_of[1]])

    blank = [jnp.zeros((head, channels), bf16), jnp.zeros((cap - head, channels), bf16)]

    def gather(i, part):
        piece_copy(i, part).wait_recv()
        top, rest = split(arrived[i, spans[part]])
        if parts == 1:
            rows_of = [top, rest]
        elif part == 0:
            rows_of = [top, blank[1], rest, blank[1]]
        else:
            rows_of = [blank[0], top, blank[0], rest]
        restricted[...] += spread(i, rows_of)

    def row_copy(side):
        return pltpu.make_async_remote_copy(
            src_ref=row_out.at[side],
            dst_ref=row_halo.at[side],
            send_sem=halo_send.at[side],
            recv_sem=halo_recv.at[side],
            device_id=(g - 1 if side else g + 1, b),
            device_id_type=MESH,
        )

    def col_copy(side):
        return pltpu.make_async_remote_copy(
            src_ref=col_out.at[side],
            dst_ref=col_halo.at[side],
            send_sem=halo_send.at[2 + side],
            recv_sem=halo_recv.at[2 + side],
            device_id=(g, b - 1 if side else b + 1),
            device_id_type=MESH,
        )

    sends = [
        (b < n_blk - 1, col_copy, 0),
        (b > 0, col_copy, 1),
        (g < n_grp - 1, row_copy, 0),
        (g > 0, row_copy, 1),
    ]
    gets = [
        (g > 0, row_copy, 0),
        (g < n_grp - 1, row_copy, 1),
        (b > 0, col_copy, 0),
        (b < n_blk - 1, col_copy, 1),
    ]

    arrivals = [2, 3, 1, 0]
    for i in arrivals:
        gather(i, 0)
    for r in range(prows):
        col_out[0, r : r + 1] = restricted[(r + 1) * pcols - 1 : (r + 1) * pcols]
        col_out[1, r : r + 1] = restricted[r * pcols : r * pcols + 1]
    row_out[0] = restricted[cells - pcols :]
    row_out[1] = restricted[:pcols]
    @pl.when(g < n_grp - 1)
    def _():
        pl.semaphore_wait(ready.at[PEERS], 1)

    for here, copy, side in sends:

        @pl.when(here)
        def _():
            copy(side).start()

    if paired:
        swap = early.astype(i32)
        restricted[...] += gather_pair(swap)
        settle()
        total = restricted[...] + gather_pair(1 - swap)
    elif parts == 2:
        settle()
        for i in arrivals:
            gather(i, 1)
    else:
        settle()

    for here, copy, side in gets:

        @pl.when(here)
        def _():
            copy(side).wait_recv()

    col = lax.rem(lax.broadcasted_iota(i32, (cells, chunk), 0), pcols)
    for c in range(channels // chunk):
        at = slice(c * chunk, (c + 1) * chunk)
        own = total[:, at] if paired else restricted[:, at]

        def widened(side):
            return jnp.broadcast_to(
                col_halo[side, :, at][:, None, :], (prows, pcols, chunk)
            ).reshape(cells, chunk)

        up = jnp.concatenate([row_halo[0, :, at], own[: cells - pcols]], axis=0)
        down = jnp.concatenate([own[pcols:], row_halo[1, :, at]], axis=0)
        left = jnp.where(col == 0, widened(0), pltpu.roll(own, 1, 0))
        right = jnp.where(col == pcols - 1, widened(1), pltpu.roll(own, cells - 1, 0))
        beside = down + up + right + left
        out_ref[:, at] = own + theta_wide[...] * (beside - 4.0 * own)

    for i in range(PEERS):
        if parts == 2:
            piece_copy(i, 1).wait_send()
    for here, copy, side in sends:

        @pl.when(here)
        def _():
            copy(side).wait_send()


def body(n_grp, n_blk, child_field, child_weight, child_slot, send_list, theta):
    children, channels = child_field.shape
    prows, pcols = theta.shape
    cells = prows * pcols
    cap = send_list.shape[1] // (PEERS + 1)
    rim = 2 * (prows + pcols) - 4
    head = min(cap, -(-rim // SUB) * SUB)
    groups = children // LANES
    f32, bf16, i32 = jnp.float32, jnp.bfloat16, jnp.int32
    dma = pltpu.SemaphoreType.DMA
    out = pl.pallas_call(
        functools.partial(kernel, n_grp, n_blk, prows, pcols, cap, head),
        out_shape=pltpu.VMEM((cells, channels), f32),
        in_specs=[pl.BlockSpec(memory_space=pltpu.HBM)] * 5,
        out_specs=pl.BlockSpec(memory_space=pltpu.VMEM),
        scratch_shapes=[
            pltpu.VMEM((children, channels), bf16),
            pltpu.VMEM((groups, LANES), bf16),
            pltpu.VMEM((groups, LANES), i32),
            pltpu.VMEM(send_list.shape, i32),
            pltpu.VMEM((prows, pcols), f32),
            pltpu.VMEM((PEERS, cap, channels), f32),
            pltpu.VMEM((PEERS, cap, channels), f32),
            pltpu.VMEM((PEERS, 1, cap), i32),
            pltpu.VMEM((PEERS, 1, cap), i32),
            pltpu.VMEM((PEERS + 1, cap, LANES), i32),
            pltpu.VMEM((2, cap, children), bf16),
            pltpu.VMEM((PEERS + 3, cells, 2 * cap), bf16),
            pltpu.VMEM((cells, channels), f32),
            pltpu.VMEM((cells, LANES), f32),
            pltpu.VMEM((2, pcols, channels), f32),
            pltpu.VMEM((2, prows, channels), f32),
            pltpu.VMEM((2, pcols, channels), f32),
            pltpu.VMEM((2, prows, channels), f32),
            dma((4 + channels // LANES,)),
            dma((PEERS,)),
            dma((PEERS,)),
            dma((PEERS, 2)),
            dma((PEERS, 2)),
            dma((4,)),
            dma((4,)),
            pltpu.SemaphoreType.REGULAR((PEERS + 1,)),
        ],
        compiler_params=pltpu.CompilerParams(
            collective_id=0, has_side_effects=True, vmem_limit_bytes=32 * 1024 * 1024
        ),
        name="nest_feedback",
    )(
        *[
            pltpu.with_memory_space_constraint(x, pltpu.HBM)
            for x in (
                child_field,
                child_weight.reshape(groups, LANES),
                child_slot.reshape(groups, LANES),
                send_list,
                theta,
            )
        ]
    )
    return out.reshape(prows, pcols, channels)


def solution(mesh):
    return jax.shard_map(
        functools.partial(body, mesh.shape["grp"], mesh.shape["blk"]),
        mesh=mesh,
        in_specs=(
            P(("grp", "blk"), None),
            P(("grp", "blk")),
            P(("grp", "blk")),
            P(("grp", "blk"), None),
            P("grp", "blk"),
        ),
        out_specs=P("grp", "blk", None),
        check_vma=False,
    )
```

```python
import functools

import jax
import jax.numpy as jnp
from jax import lax
from jax.experimental import pallas as pl
from jax.experimental.pallas import tpu as pltpu
from jax.sharding import PartitionSpec as P

HALF = 2
PEERS = 2 * HALF
LANES = 128
SUB = 16
MESH = pl.DeviceIdType.MESH


def kernel(
    n_grp,
    n_blk,
    prows,
    pcols,
    cap,
    head,
    field_hbm,
    weight_hbm,
    slot_hbm,
    list_hbm,
    theta_hbm,
    out_ref,
    field,
    weight,
    slot,
    lists,
    theta,
    pieces,
    arrived,
    ordered,
    numbers,
    wanted,
    weighted,
    selector,
    restricted,
    theta_wide,
    row_out,
    col_out,
    row_halo,
    col_halo,
    in_sem,
    num_send,
    num_recv,
    piece_send,
    piece_recv,
    halo_send,
    halo_recv,
    ready,
):
    g = lax.axis_index("grp")
    b = lax.axis_index("blk")
    cells = prows * pcols
    children, channels = field.shape
    chunk = LANES
    parts = 2 if head < cap else 1
    f32, bf16, i32 = jnp.float32, jnp.bfloat16, jnp.int32
    early = b < HALF
    late = b >= n_blk - HALF

    def offset(i):
        if isinstance(i, int):
            return i - HALF + (i >= HALF)
        return i - HALF + (i >= HALF).astype(i32)

    def peer(i):
        return (g, lax.rem(b + offset(i) + n_blk, n_blk))

    turn = jnp.where(b == 0, 2, 0) + jnp.where(b == 1, 1, 0)
    turn = turn + jnp.where(b == n_blk - 2, 3, 0) + jnp.where(b == n_blk - 1, 2, 0)

    def nth(j):
        i = lax.rem(turn + j, PEERS)
        alt = [0, HALF, HALF + 1, 1][j]
        i = jnp.where(b == n_blk - 2, [0, 3, 1, 2][j], i)
        return jnp.where((b == n_blk - 1) & (lax.rem(g, 2) == 1), alt, i)

    def above(i):
        return lax.rem(b + offset(i) + n_blk, n_blk) > b

    small = [
        pltpu.make_async_copy(src, dst, in_sem.at[i])
        for i, (src, dst) in enumerate(
            [(list_hbm, lists), (slot_hbm, slot), (weight_hbm, weight), (theta_hbm, theta)]
        )
    ]
    large = [
        pltpu.make_async_copy(
            field_hbm.at[:, pl.ds(q * chunk, chunk)],
            field.at[:, pl.ds(q * chunk, chunk)],
            in_sem.at[len(small) + q],
        )
        for q in range(channels // chunk)
    ]
    for load in [*small[:3], *large, small[3]]:
        load.start()

    barrier = pltpu.get_barrier_semaphore()
    greeted = (g > 0).astype(i32)
    for i in range(PEERS):

        @pl.when(above(i))
        def _():
            pl.semaphore_signal(barrier, inc=1, device_id=peer(i), device_id_type=MESH)

        greeted += 1 - above(i).astype(i32)

    @pl.when(g < n_grp - 1)
    def _():
        pl.semaphore_signal(barrier, inc=1, device_id=(g + 1, b), device_id_type=MESH)

    @pl.when(g == 0)
    def _():
        row_halo[0] = jnp.zeros_like(row_halo[0])

    @pl.when(g == n_grp - 1)
    def _():
        row_halo[1] = jnp.zeros_like(row_halo[1])

    @pl.when(b == 0)
    def _():
        col_halo[0] = jnp.zeros_like(col_halo[0])

    @pl.when(b == n_blk - 1)
    def _():
        col_halo[1] = jnp.zeros_like(col_halo[1])

    small[0].wait()
    lane = lax.broadcasted_iota(i32, (cap, cap), 1)
    sub = lax.broadcasted_iota(i32, (cap, cap), 0)
    owned = [0, 1, 3, 4]
    table = jnp.concatenate(
        [lists[:, k * cap : (k + 1) * cap] for k in owned]
        + [jnp.full((SUB - PEERS, cap), -1, i32)],
        axis=0,
    )
    place = lax.rem(table, pcols)
    rim = (table < pcols) | (table >= cells - pcols) | (place == 0) | (place == pcols - 1)
    rim = rim & (table >= 0)
    ones = jnp.where(rim, 1.0, 0.0)
    before = jnp.dot(
        ones.astype(bf16), jnp.where(sub < lane, 1.0, 0.0).astype(bf16), preferred_element_type=f32
    )
    count = jnp.sum(ones, axis=1, keepdims=True)
    own_lane = lax.broadcasted_iota(i32, (SUB, cap), 1).astype(f32)
    position = jnp.where(rim, before, count + own_lane - before).astype(i32)
    high, low = table[:8] >> 7, table[:8] & 127
    halves = jnp.concatenate([high, low], axis=0).astype(f32).astype(bf16)
    for i in range(PEERS):
        goes = position[i : i + 1, :] == sub
        source = jnp.sum(jnp.where(goes, lane, 0), axis=1, keepdims=True)
        wanted[i] = jnp.broadcast_to(source + owned[i] * cap, (cap, LANES))
        moved = lax.dot_general(
            halves,
            jnp.where(goes, 1.0, 0.0).astype(bf16),
            (((1,), (1,)), ((), ())),
            preferred_element_type=f32,
        ).astype(i32)
        ordered[i] = moved[i : i + 1, :] * 128 + moved[8 + i : 9 + i, :]
    wanted[PEERS] = sub + HALF * cap

    small[1].wait()
    small[2].wait()
    slots = slot[...]
    weights = weight[...].astype(f32)

    def weigh(i, at):
        ids = wanted[i]
        for j in range(children // LANES):
            hit = jnp.where(ids == slots[j : j + 1, :], weights[j : j + 1, :], 0.0)
            weighted[at, :, j * LANES : (j + 1) * LANES] = hit.astype(bf16)

    def number_copy(i):
        return pltpu.make_async_remote_copy(
            src_ref=ordered.at[i],
            dst_ref=numbers.at[i],
            send_sem=num_send.at[i],
            recv_sem=num_recv.at[i],
            device_id=peer(i),
            device_id_type=MESH,
        )

    spans = [pl.ds(0, head), pl.ds(head, cap - head)]

    def piece_copy(i, part):
        return pltpu.make_async_remote_copy(
            src_ref=pieces.at[i, spans[part]],
            dst_ref=arrived.at[i, spans[part]],
            send_sem=piece_send.at[i, part],
            recv_sem=piece_recv.at[i, part],
            device_id=peer(i),
            device_id_type=MESH,
        )

    def first_copy(i, start):
        at = pl.ds(start, chunk)
        return pltpu.make_async_remote_copy(
            src_ref=pieces.at[i, spans[0], at],
            dst_ref=arrived.at[i, spans[0], at],
            send_sem=piece_send.at[i, 0],
            recv_sem=piece_recv.at[i, 0],
            device_id=peer(i),
            device_id_type=MESH,
        )

    def tail(j):
        if parts == 2:
            piece_copy(nth(j), 1).start()

    @pl.when(greeted > 0)
    def _():
        pl.semaphore_wait(barrier, greeted)

    for q in range(PEERS):

        @pl.when(~above(q))
        def _():
            pl.semaphore_signal(
                ready.at[q], inc=1, device_id=peer(q), device_id_type=MESH
            )

    @pl.when(g > 0)
    def _():
        pl.semaphore_signal(
            ready.at[PEERS], inc=1, device_id=(g - 1, b), device_id_type=MESH
        )

    weigh(nth(0), 0)
    for j in range(PEERS):
        i = nth(j)
        if j > 0:
            weigh(i, j % 2)
            pieces[i] = jnp.dot(weighted[j % 2], field[...], preferred_element_type=f32)

        @pl.when(above(i))
        def _():
            pl.semaphore_wait(ready.at[PEERS - 1 - i], 1)

        number_copy(i).start()
        if j > 0:
            piece_copy(i, 0).start()
        else:
            for q, load in enumerate(large):
                load.wait()
                at = slice(q * chunk, (q + 1) * chunk)
                pieces[i, :, at] = jnp.dot(weighted[0], field[:, at], preferred_element_type=f32)
                first_copy(i, q * chunk).start()
        if j == 1:

            @pl.when((b == n_blk - 1) & (g == 0))
            def _():
                tail(0)

    last = ((b == n_blk - 1) & (lax.rem(g, 2) == 1)) | (b == n_blk - 2)

    @pl.when(~((b == n_blk - 1) & (g == 0)) & ~last)
    def _():
        tail(0)

    tail(1)
    tail(2)

    @pl.when(last)
    def _():
        tail(0)

    tail(3)

    def select(i, entries):
        hit = lax.broadcasted_iota(i32, (cells, cap), 0) == entries
        hit = jnp.where(hit, 1.0, 0.0).astype(bf16)
        selector[i] = jnp.concatenate([hit, hit], axis=1)

    def split(piece):
        top = piece.astype(bf16)
        return top, (piece - top.astype(f32)).astype(bf16)

    def spread(i, rows_of):
        return jnp.dot(selector[i], jnp.concatenate(rows_of, axis=0), preferred_element_type=f32)

    select(PEERS, lists[:, HALF * cap : (HALF + 1) * cap])
    weigh(PEERS, 0)
    made = jnp.dot(weighted[0], field[...], preferred_element_type=f32)
    restricted[...] = spread(PEERS, split(made))

    small[3].wait()
    diagonal = lax.broadcasted_iota(i32, (pcols, pcols), 0) == lax.broadcasted_iota(
        i32, (pcols, pcols), 1
    )
    for r in range(prows):
        column = jnp.sum(jnp.where(diagonal, theta[r : r + 1, :], 0.0), axis=1, keepdims=True)
        theta_wide[r * pcols : (r + 1) * pcols, :] = jnp.broadcast_to(column, (pcols, chunk))

    for i in range(PEERS):
        number_copy(i).wait_recv()
        select(i, numbers[i])

    rest = cap - head
    paired = parts == 2 and rest <= head
    if paired:
        lane8 = lax.broadcasted_iota(i32, (8, cap), 1)
        for p in range(2):
            first = jnp.broadcast_to(numbers[2 - p], (8, cap))
            second = pltpu.roll(jnp.broadcast_to(numbers[3 - 3 * p], (8, cap)), cap - rest, 1)
            both = jnp.where(lane8 >= head, first, jnp.where(lane8 >= head - rest, second, -1))
            select(PEERS + 1 + p, both[:1])

    def settle():
        for i in range(PEERS):
            number_copy(i).wait_send()
            piece_copy(i, 0).wait_send()

    def gather_pair(p):
        rows_of = [[], []]
        for i in (3 - 3 * p, 2 - p):
            piece_copy(i, 1).wait_recv()
            for side, value in enumerate(split(arrived[i, spans[1]])):
                rows_of[side].append(value)
        if head > rest:
            gap = [jnp.zeros((head - rest, channels), bf16)]
        else:
            gap = []
        return spread(PEERS + 1 + p, [*gap, *rows_of[0], *gap, *rows_of[1]])

    blank = [jnp.zeros((head, channels), bf16), jnp.zeros((cap - head, channels), bf16)]

    def gather(i, part):
        piece_copy(i, part).wait_recv()
        top, rest = split(arrived[i, spans[part]])
        if parts == 1:
            rows_of = [top, rest]
        elif part == 0:
            rows_of = [top, blank[1], rest, blank[1]]
        else:
            rows_of = [blank[0], top, blank[0], rest]
        restricted[...] += spread(i, rows_of)

    def row_copy(side):
        return pltpu.make_async_remote_copy(
            src_ref=row_out.at[side],
            dst_ref=row_halo.at[side],
            send_sem=halo_send.at[side],
            recv_sem=halo_recv.at[side],
            device_id=(g - 1 if side else g + 1, b),
            device_id_type=MESH,
        )

    def col_copy(side):
        return pltpu.make_async_remote_copy(
            src_ref=col_out.at[side],
            dst_ref=col_halo.at[side],
            send_sem=halo_send.at[2 + side],
            recv_sem=halo_recv.at[2 + side],
            device_id=(g, b - 1 if side else b + 1),
            device_id_type=MESH,
        )

    sends = [
        (b < n_blk - 1, col_copy, 0),
        (b > 0, col_copy, 1),
        (g < n_grp - 1, row_copy, 0),
        (g > 0, row_copy, 1),
    ]
    gets = [
        (g > 0, row_copy, 0),
        (g < n_grp - 1, row_copy, 1),
        (b > 0, col_copy, 0),
        (b < n_blk - 1, col_copy, 1),
    ]

    arrivals = [2, 3, 1, 0]
    for i in arrivals:
        gather(i, 0)
    for r in range(prows):
        col_out[0, r : r + 1] = restricted[(r + 1) * pcols - 1 : (r + 1) * pcols]
        col_out[1, r : r + 1] = restricted[r * pcols : r * pcols + 1]
    row_out[0] = restricted[cells - pcols :]
    row_out[1] = restricted[:pcols]
    @pl.when(g < n_grp - 1)
    def _():
        pl.semaphore_wait(ready.at[PEERS], 1)

    for here, copy, side in sends:

        @pl.when(here)
        def _():
            copy(side).start()

    if paired:
        swap = early.astype(i32)
        restricted[...] += gather_pair(swap)
        settle()
        total = restricted[...] + gather_pair(1 - swap)
    elif parts == 2:
        settle()
        for i in arrivals:
            gather(i, 1)
    else:
        settle()

    for here, copy, side in gets:

        @pl.when(here)
        def _():
            copy(side).wait_recv()

    col = lax.rem(lax.broadcasted_iota(i32, (cells, chunk), 0), pcols)
    for c in range(channels // chunk):
        at = slice(c * chunk, (c + 1) * chunk)
        own = total[:, at] if paired else restricted[:, at]

        def widened(side):
            return jnp.broadcast_to(
                col_halo[side, :, at][:, None, :], (prows, pcols, chunk)
            ).reshape(cells, chunk)

        up = jnp.concatenate([row_halo[0, :, at], own[: cells - pcols]], axis=0)
        down = jnp.concatenate([own[pcols:], row_halo[1, :, at]], axis=0)
        left = jnp.where(col == 0, widened(0), pltpu.roll(own, 1, 0))
        right = jnp.where(col == pcols - 1, widened(1), pltpu.roll(own, cells - 1, 0))
        beside = down + up + right + left
        out_ref[:, at] = own + theta_wide[...] * (beside - 4.0 * own)

    for i in range(PEERS):
        if parts == 2:
            piece_copy(i, 1).wait_send()
    for here, copy, side in sends:

        @pl.when(here)
        def _():
            copy(side).wait_send()


def body(n_grp, n_blk, child_field, child_weight, child_slot, send_list, theta):
    children, channels = child_field.shape
    prows, pcols = theta.shape
    cells = prows * pcols
    cap = send_list.shape[1] // (PEERS + 1)
    rim = 2 * (prows + pcols) - 4
    head = min(cap, -(-rim // SUB) * SUB)
    groups = children // LANES
    f32, bf16, i32 = jnp.float32, jnp.bfloat16, jnp.int32
    dma = pltpu.SemaphoreType.DMA
    out = pl.pallas_call(
        functools.partial(kernel, n_grp, n_blk, prows, pcols, cap, head),
        out_shape=pltpu.VMEM((cells, channels), f32),
        in_specs=[pl.BlockSpec(memory_space=pltpu.HBM)] * 5,
        out_specs=pl.BlockSpec(memory_space=pltpu.VMEM),
        scratch_shapes=[
            pltpu.VMEM((children, channels), bf16),
            pltpu.VMEM((groups, LANES), bf16),
            pltpu.VMEM((groups, LANES), i32),
            pltpu.VMEM(send_list.shape, i32),
            pltpu.VMEM((prows, pcols), f32),
            pltpu.VMEM((PEERS, cap, channels), f32),
            pltpu.VMEM((PEERS, cap, channels), f32),
            pltpu.VMEM((PEERS, 1, cap), i32),
            pltpu.VMEM((PEERS, 1, cap), i32),
            pltpu.VMEM((PEERS + 1, cap, LANES), i32),
            pltpu.VMEM((2, cap, children), bf16),
            pltpu.VMEM((PEERS + 3, cells, 2 * cap), bf16),
            pltpu.VMEM((cells, channels), f32),
            pltpu.VMEM((cells, LANES), f32),
            pltpu.VMEM((2, pcols, channels), f32),
            pltpu.VMEM((2, prows, channels), f32),
            pltpu.VMEM((2, pcols, channels), f32),
            pltpu.VMEM((2, prows, channels), f32),
            dma((4 + channels // LANES,)),
            dma((PEERS,)),
            dma((PEERS,)),
            dma((PEERS, 2)),
            dma((PEERS, 2)),
            dma((4,)),
            dma((4,)),
            pltpu.SemaphoreType.REGULAR((PEERS + 1,)),
        ],
        compiler_params=pltpu.CompilerParams(
            collective_id=0, has_side_effects=True, vmem_limit_bytes=32 * 1024 * 1024
        ),
        name="nest_feedback",
    )(
        *[
            pltpu.with_memory_space_constraint(x, pltpu.HBM)
            for x in (
                child_field,
                child_weight.reshape(groups, LANES),
                child_slot.reshape(groups, LANES),
                send_list,
                theta,
            )
        ]
    )
    return out.reshape(prows, pcols, channels)


def solution(mesh):
    return jax.shard_map(
        functools.partial(body, mesh.shape["grp"], mesh.shape["blk"]),
        mesh=mesh,
        in_specs=(
            P(("grp", "blk"), None),
            P(("grp", "blk")),
            P(("grp", "blk")),
            P(("grp", "blk"), None),
            P("grp", "blk"),
        ),
        out_specs=P("grp", "blk", None),
        check_vma=False,
    )
```
